256 devices in a mesh: gx: 4 (over x), gy: 8 (over z), gz: 8 (over y, core).
Axes of the slice: x: 4, y: 4, z: 8, core: 2. Of those that a mesh axis runs over, the one named last changes fastest.
Arguments:
- nodal_field: float32 [128, 1024, 2048], P('gx', 'gy', 'gz'), may hold values from -6 to 6
- spacing_x: float32 [128], replicated, may hold values from 0.5 to 2
- spacing_z: float32 [2048], replicated, may hold values from 0.5 to 2
- operator_x: float32 [64, 16], P('gx'), may hold values from -1.5 to 1.5
- persist_x: float32 [64], P('gx'), may hold values from 0.6 to 1
- operator_z: float32 [1024, 128], P('gz'), may hold values from -0.5 to 0.5
- persist_z: float32 [1024], P('gz'), may hold values from 0.6 to 1
- receivers: int32 [131072, 1], P(('gx', 'gy', 'gz')), may hold values from 0 to 63; in each aligned block of 512 rows (0 to 511, 512 to 1023, ...) at most 16 rows name the same one
Outputs:
- detail_x: float32 [64, 1024, 2048], P('gx', 'gy', 'gz')
- detail_z: float32 [64, 1024, 1024], P('gx', 'gy', 'gz')
- received: float32 [256, 64, 16, 2, 4, 128], P(('gx', 'gy', 'gz'))
The draws below stay inside these ranges and needn't reach their ends.
Inputs may be any that keep to these rules, and one draw needn't show every extreme that they name: `receivers`: each row names the receiving device of one kept block among the 64 devices with the same gx index, in (gy, gz) row-major order; of the 512 blocks of one device at most 16 name the same receiver, and that bound is reached.
All inputs are finite; a program needn't handle non-finite values.
Results may differ from the reference program's by a relative error of at most 0.00008.
Values sent between devices are 32-bit elements; how exact they have to be, the bound alone decides.
No kernel may reach another device: no remote copies, remote signals or barrier semaphores. Data moves between devices by JAX's collectives and lax.ppermute only.
A program may use at most 64 MiB of HBM per device.

```python
import math
import jax
import jax.numpy as jnp
import numpy as np
from jax import lax

CY = 128
LINES = 4
HX = 16
HZ = 128
NB = 512
MOST = 16
NX = 128
NY = 1024
NZ = 2048
N_GX = 4
N_GY = 8
N_GZ = 8
DEVICES = 256


def block_scale(key, dims, shards, least, largest):
    def one(position, blocks):
        heights = jax.random.uniform(jax.random.fold_in(jax.random.fold_in(key, 6), position), (blocks,), jnp.float32, least / len(shards), largest / len(shards))
        return jnp.repeat(jnp.exp(heights), dims[position] // blocks).reshape((-1,) + (1,) * (len(dims) - position - 1))

    gain = one(*shards[0])
    for cut in shards[1:]:
        gain = gain * one(*cut)
    return gain


def deal_out(key, own, number, rows, amount, top, reach, slope):
    order = jax.random.permutation(key, amount)
    heavy_load, common = portions_of(amount, rows * top, reach, slope, True), portions_of(amount, rows * top, reach, slope, False)
    places = jnp.arange(amount)

    def named(tallies, offset_by):
        used = int((tallies > 0).sum())
        fixed = max(1, used // 4)
        moved = fixed + (places - fixed + offset_by * (used - fixed)) % max(1, amount - fixed)
        return jnp.zeros((amount,), jnp.int32).at[order[jnp.where(places < fixed, places, moved)]].set(jnp.asarray(tallies, jnp.int32))

    tallies = jnp.where(number % 4 == 0, named(heavy_load, number // 4), named(common, number - number // 4 - 1))
    mixed = jax.random.permutation(jax.random.fold_in(own, 3), amount)
    source_of, taker = mixed[0:amount // 2 * 2:2], mixed[1:amount // 2 * 2:2]
    room = jnp.minimum(tallies[source_of] - 1, reach - tallies[taker]) // 2
    room = jnp.where((source_of == order[0]) | (taker == order[0]) | (tallies[taker] == 0), 0, jnp.maximum(room, 0))
    moved = jax.random.randint(jax.random.fold_in(own, 4), (amount // 2,), 0, 1 << 20) % (room + 1)
    tallies = tallies.at[source_of].add(-moved).at[taker].add(moved)
    members = jnp.searchsorted(jnp.cumsum(tallies), jnp.arange(rows * top), side="right").astype(jnp.int32)
    listing = members.reshape(top, rows).T
    listing = listing[jax.random.permutation(jax.random.fold_in(own, 1), rows)]
    offset_by = jax.random.randint(jax.random.fold_in(own, 2), (rows, 1), 0, top)
    return jnp.take_along_axis(listing, (jnp.arange(top)[None, :] + offset_by) % top, axis=1)


def portions_of(number_of, total, most, lean, full):
    portions = [(1 << 20) // math.isqrt(standing ** lean) + 1 for standing in range(1, number_of + 1)]
    largest = most if full else min(most, max(-(-total // number_of), total * portions[0] // sum(portions)))
    least = 1 if total - largest >= number_of - 1 else 0
    holding, rest = [largest] + [least] * (number_of - 1), total - largest - least * (number_of - 1)
    while rest > 0:
        free = [i for i in range(1, number_of) if holding[i] < largest] or [i for i in range(1, number_of) if holding[i] < most]
        whole, left = sum([portions[i] for i in free]), rest
        for i in free:
            more = min(most - holding[i], max(1, left * portions[i] // whole), rest)
            holding[i] = holding[i] + more
            rest = rest - more
    return np.array(holding)


def centred(own_key, dims, scale, limit, cuts=(), kind=jnp.bfloat16):
    result = jax.random.normal(own_key, dims, jnp.float32) * scale
    if len(cuts) > 0:
        result = block_scale(own_key, dims, cuts, -0.22, 0.18) * result
    return jnp.clip(result, min=-limit, max=limit).astype(kind)


def setup_inputs(seed: int = 0) -> dict:
    keys = jax.random.split(jax.random.key(seed), 9)
    nodal_field = centred(keys[0], (NX, NY, NZ), 1.0, 6.0, ((0, 4), (1, 8), (2, 8)), jnp.float32)
    spacing_x = jnp.clip(jnp.exp(jax.random.uniform(keys[1], (NX,), jnp.float32, math.log(0.5), math.log(2.0))), 0.5, 2.0)
    spacing_z = jnp.clip(jnp.exp(jax.random.uniform(keys[2], (NZ,), jnp.float32, math.log(0.5), math.log(2.0))), 0.5, 2.0)
    operator_x = centred(keys[3], (NX // 2, HX), HX ** -0.5, 1.5, ((0, 4),), jnp.float32)
    persist_x = jnp.clip(0.6 + 0.39999998 * jax.random.uniform(keys[4], (NX // 2,), jnp.float32) ** block_scale(keys[4], (NX // 2,), ((0, 4),), -0.2, 0.2), 0.6, 1.0)
    operator_z = centred(keys[5], (NZ // 2, HZ), HZ ** -0.5, 0.5, ((0, 8),), jnp.float32)
    persist_z = jnp.clip(0.6 + 0.39999998 * jax.random.uniform(keys[6], (NZ // 2,), jnp.float32) ** block_scale(keys[6], (NZ // 2,), ((0, 8),), -0.2, 0.2), 0.6, 1.0)
    receivers_keys = jax.random.split(jax.random.fold_in(keys[7], 1), (DEVICES * NB) // NB)
    receivers_turns = jax.random.permutation(jax.random.fold_in(keys[7], 3), (DEVICES * NB) // NB)
    receivers = jax.vmap(lambda own, number: deal_out(jax.random.fold_in(keys[7], 2), own, number, NB, N_GY * N_GZ, 1, MOST, 2))(receivers_keys, receivers_turns).reshape((DEVICES * NB, 1))
    return dict(nodal_field=nodal_field, spacing_x=spacing_x, spacing_z=spacing_z, operator_x=operator_x, persist_x=persist_x, operator_z=operator_z, persist_z=persist_z, receivers=receivers)


def refine(nodes, spacing, row_blocks, gain_list, parts):
    length = nodes.shape[0]
    coarse_count = length // 2
    block_len = coarse_count // parts
    space_even = spacing[0::2]
    space_odd = spacing[1::2]
    span_sum = space_even + space_odd
    weight_a = (space_odd / span_sum)[:, None, None]
    weight_b = (space_even / span_sum)[:, None, None]
    even_nodes = nodes[0::2]
    odd_nodes = nodes[1::2]
    right_nodes = jnp.concatenate([even_nodes[1:], jnp.zeros_like(even_nodes[:1])], 0)
    detail = odd_nodes - weight_a * even_nodes - weight_b * right_nodes
    near_terms = (0.5 * space_even)[:, None, None] * detail
    far_terms = (0.5 * space_odd)[:, None, None] * detail
    load_terms = near_terms + jnp.concatenate([jnp.zeros_like(far_terms[:1]), far_terms[:-1]], 0)
    line_count = load_terms.shape[1] * load_terms.shape[2]
    grouped = load_terms.reshape(parts, block_len, line_count)
    operators = row_blocks.reshape(parts, block_len, block_len)
    local_part = jnp.einsum("pij,pjm->pim", operators, grouped, precision=lax.Precision.HIGHEST)
    gain_blocks = gain_list.reshape(parts, block_len, 1)
    carried = jnp.zeros_like(local_part[0, 0])
    pieces = []
    for member in range(parts):
        solved = local_part[member] + gain_blocks[member] * carried[None, :]
        pieces.append(solved)
        carried = solved[-1]
    solved_all = jnp.stack(pieces, 0).reshape(load_terms.shape)
    return detail, even_nodes + solved_all


def reference(nodal_field, spacing_x, spacing_z, operator_x, persist_x, operator_z, persist_z, receivers):
    detail_x, coarse_x = refine(nodal_field, spacing_x, operator_x, persist_x, N_GX)
    moved_detail, moved_coarse = refine(jnp.moveaxis(coarse_x, 2, 0), spacing_z, operator_z, persist_z, N_GZ)
    detail_z = jnp.moveaxis(moved_detail, 0, 2)
    coarse_z = jnp.moveaxis(moved_coarse, 0, 2)
    group_size = N_GY * N_GZ
    device_count = N_GX * group_size

    def bricks(array):
        shaped = array.reshape(N_GX, HX, N_GY, CY, N_GZ, HZ).transpose(0, 2, 4, 1, 3, 5)
        return shaped.reshape(device_count, NB, LINES, HZ)

    tile_rows = jnp.stack([bricks(coarse_z), bricks(detail_z)], 2)
    targets = receivers.reshape(device_count, NB).astype(jnp.int32)
    positions = jnp.arange(NB, dtype=jnp.int32)
    earlier = (targets[:, None, :] == targets[:, :, None]) & (positions[None, None, :] < positions[None, :, None])
    slots = jnp.sum(earlier.astype(jnp.int32), axis=2).astype(jnp.int32)
    senders = jnp.broadcast_to(jnp.arange(device_count, dtype=jnp.int32)[:, None], targets.shape)
    outgoing = jnp.zeros((device_count, group_size * MOST, 2, LINES, HZ), jnp.float32)
    outgoing = outgoing.at[senders, targets * MOST + slots].set(tile_rows)
    arranged = outgoing.reshape(N_GX, group_size, group_size, MOST, 2, LINES, HZ).transpose(0, 2, 1, 3, 4, 5, 6)
    return detail_x, detail_z, arranged.reshape(device_count, group_size, MOST, 2, LINES, HZ)
```

```python
import jax
import jax.numpy as jnp
from jax import lax
from jax.experimental import pallas as pl
from jax.experimental.pallas import tpu as pltpu
from jax.sharding import PartitionSpec as P

LINES = 4
F32 = jnp.float32
BF16 = jnp.bfloat16
SMEM = pltpu.SMEM
VMEM = pltpu.VMEM
LIMIT = 48 * 1024 * 1024


def spec(space):
    return pl.BlockSpec(memory_space=space)


def cost(flops, moved):
    return pl.CostEstimate(flops=flops, bytes_accessed=moved, transcendentals=0)


def params():
    return pltpu.CompilerParams(vmem_limit_bytes=LIMIT)


def ratio(top, bottom):
    return jnp.full((1, 1), top, F32) / jnp.full((1, 1), bottom, F32)


def weights_x(rank_ref, h_ref, k):
    base = rank_ref[0] * 32 + 2 * k
    if k < 0:
        base = jnp.maximum(base, 0)
    even, odd = h_ref[base], h_ref[base + 1]
    total = even + odd
    near, far = 0.5 * even, 0.5 * odd
    if k < 0:
        far = jnp.where(rank_ref[0] > 0, far, 0.0)
    return ratio(odd, total), ratio(even, total), near, far


def edge_kernel(rank_ref, h_ref, low_ref, high_ref, first_ref, last_ref):
    a, _, _, _ = weights_x(rank_ref, h_ref, 15)
    first_ref[...] = low_ref[0]
    last_ref[...] = high_ref[1] - a * high_ref[0]


def tail_kernel(rank_ref, h_ref, f_ref, x_ref, out_ref):
    _, b_before, _, far_before = weights_x(rank_ref, h_ref, -1)
    before = -f_ref[15, 0] * far_before * b_before
    total = None
    for j in range(16):
        a, b, near, far = weights_x(rank_ref, h_ref, j)
        v = f_ref[15, j] * near
        if j < 15:
            v = v + f_ref[15, j + 1] * far
        term = (before - v * a) * x_ref[2 * j] + v * x_ref[2 * j + 1]
        total = term if total is None else total + term
        before = -v * b
    out_ref[...] = total


def close_kernel(rank_ref, h_ref, f_ref, g_ref, own_ref, right_ref, left_ref, out_ref):
    _, b, near, _ = weights_x(rank_ref, h_ref, 15)
    _, _, _, far = weights_x(rank_ref, h_ref, -1)
    alpha = -(f_ref[15, 15] * near) * b
    beta = f_ref[15, 0] * far
    out_ref[0:128, :] = own_ref[...] + alpha * right_ref[...] + beta * left_ref[...]
    out_ref[128:136, :] = jnp.full((8, 256), g_ref[15], F32)


def split(value):
    high = value.astype(BF16)
    return high, (value - high.astype(F32)).astype(BF16)


def dot3(value, high, low):
    v_high, v_low = split(value)
    one = lambda a, b: jnp.dot(a, b, preferred_element_type=F32)
    return one(v_high, high) + (one(v_low, high) + one(v_high, low))


def table_kernel(rank_ref, h_ref, even_ref, odd_ref, f_ref, g_ref, high_ref, low_ref, row_ref):
    even, odd = even_ref[...], odd_ref[...]
    total = even + odd
    a, b = odd / total, even / total
    near, far = 0.5 * even, 0.5 * odd
    at = jnp.maximum(rank_ref[0] * 256 - 2, 0)
    h_even, h_odd = h_ref[at], h_ref[at + 1]
    far_before = jnp.where(rank_ref[0] > 0, 0.5 * h_odd, 0.0)
    b_before = ratio(h_even, h_even + h_odd)
    z = lax.broadcasted_iota(jnp.int32, (256, 128), 0)
    k = lax.broadcasted_iota(jnp.int32, (256, 128), 1)
    chosen = jnp.where(z == 2 * k, 1.0, 0.0)
    detail = jnp.where(z == 2 * k + 1, 1.0, 0.0) - chosen * a - jnp.where(z == 2 * k + 2, b, 0.0)
    shifted = jnp.where(k == 0, 0.0, pltpu.roll(detail * far, 1, 1))
    load = detail * near + shifted
    load = load - jnp.where((z == 0) & (k == 0), far_before * b_before, 0.0)
    contract = (((1,), (1,)), ((), ()))
    coarse = chosen + lax.dot_general(
        load, f_ref[...], contract, precision=lax.Precision.HIGHEST, preferred_element_type=F32
    )
    high, low = split(detail)
    high_ref[:, 0:128], low_ref[:, 0:128] = high, low
    high, low = split(coarse)
    high_ref[:, 128:256], low_ref[:, 128:256] = high, low
    row = lax.broadcasted_iota(jnp.int32, (8, 128), 0)
    lane = lax.broadcasted_iota(jnp.int32, (8, 128), 1)
    pick = jnp.where(((row == 1) & (lane == 127)) | ((row == 2) & (lane == 0)), 1.0, 0.0)
    columns = lax.dot_general(
        pick, f_ref[...], contract, precision=lax.Precision.HIGHEST, preferred_element_type=F32
    )
    last = lane[0:1] == 127
    b_last = jnp.sum(jnp.where(last, b, 0.0), axis=1, keepdims=True)
    near_last = jnp.sum(jnp.where(last, near, 0.0), axis=1, keepdims=True)
    end = lambda v: jnp.broadcast_to(jnp.sum(jnp.where(last, v, 0.0), axis=1, keepdims=True), (1, 128))
    from_right = columns[1:2] * (-near_last * b_last)
    from_left = columns[2:3] * far_before
    gain = g_ref[...]
    row_ref[0:1] = jnp.where(last, -b, 0.0)
    row_ref[1:2] = from_right
    row_ref[2:3] = from_left
    row_ref[3:4] = gain
    row_ref[4:5] = end(from_right)
    row_ref[5:6] = end(from_left)
    row_ref[6:7] = end(gain)
    row_ref[7:8] = jnp.zeros((1, 128), F32)


def main_kernel(
    rank_ref, h_ref, f_ref, x_ref, right_ref, left_ref, high_ref, low_ref,
    detail_ref, dz_ref, cz_ref, column_ref, w_ref, v_ref,
):
    @pl.when(pl.program_id(0) == 0)
    def _():
        for k in range(-1, 16):
            for i, value in enumerate(weights_x(rank_ref, h_ref, k)):
                w_ref[i, k + 1] = jnp.broadcast_to(value, (8, 128))

    def weight(i, k):
        one = w_ref[i, k + 1]
        return jnp.concatenate([one, one], axis=1)

    def body(step, _):
        rows = pl.ds(pl.multiple_of(step * 8, 8), 8)
        loads = []
        x_even = x_ref[0, rows, :]
        carried = weight(3, -1) * (left_ref[rows, :] - weight(1, -1) * x_even)
        for j in range(16):
            x_odd = x_ref[2 * j + 1, rows, :]
            x_next = x_ref[2 * j + 2, rows, :] if j < 15 else right_ref[rows, :]
            detail = x_odd - weight(0, j) * x_even - weight(1, j) * x_next
            detail_ref[j, rows, :] = detail
            loads.append(weight(2, j) * detail + carried)
            carried = weight(3, j) * detail
            x_even = x_next
        for k in range(16):
            parts = [f_ref[k, j] * loads[j] for j in range(16)]
            while len(parts) > 1:
                parts = [parts[i] + parts[i + 1] for i in range(0, len(parts), 2)]
            v_ref[k, rows, :] = x_ref[2 * k, rows, :] + parts[0]
        return 0

    chunk = x_ref.shape[1]
    lax.fori_loop(0, chunk // 8, body, 0)
    values = v_ref[...].reshape(16 * chunk, 256)
    both = dot3(values, high_ref[...], low_ref[...])
    both = both.reshape(16, chunk, 256)
    dz_ref[...] = both[:, :, 0:128]
    cz_ref[...] = both[:, :, 128:256]
    lane = lax.broadcasted_iota(jnp.int32, (chunk, 128), 1)
    message = jnp.zeros((chunk, 128), F32)
    spread = lambda column: jnp.broadcast_to(column, (chunk, 128))
    for k in range(16):
        message = jnp.where(lane == k, spread(v_ref[k, :, 0:1]), message)
        message = jnp.where(lane == 16 + k, spread(dz_ref[k, :, 127:128]), message)
        tail = cz_ref[k, :, 127:128] - v_ref[k, :, 254:255]
        message = jnp.where(lane == 32 + k, spread(tail), message)
    column_ref[...] = message


def carry_kernel(g_ref, one_ref, two_ref, three_ref, high_ref, low_ref, row_ref, column_ref, plane_ref, out_ref):
    carry = two_ref[0:128, :] + two_ref[128:129, :] * three_ref[0:128, :]
    carry = one_ref[0:128, :] + one_ref[128:129, :] * carry
    plane = dot3(carry, high_ref[...], low_ref[...])
    plane_ref[...] = plane
    lane = lax.broadcasted_iota(jnp.int32, (1, 128), 1)
    gain = jnp.zeros((1, 128), F32)
    for k in range(48):
        gain = jnp.where(lane == k, g_ref[k % 16], gain)
    spread = lambda column: jnp.broadcast_to(column, (128, 128))
    wide = lax.broadcasted_iota(jnp.int32, (128, 128), 1)
    pieces = jnp.where(
        wide < 16,
        spread(carry[:, 0:1]),
        jnp.where(wide < 32, spread(plane[:, 127:128]), spread(plane[:, 255:256] - carry[:, 254:255])),
    )
    message = column_ref[...] + gain * pieces
    for i in range(3):
        message = jnp.where(wide == 48 + i, row_ref[4 + i : 5 + i, :], message)
    out_ref[...] = message


def last_kernel(
    rank_ref, g_ref, place_ref, dz_ref, cz_ref, plane_ref, all_ref, row_ref, detail_ref, out_ref
):
    rank = rank_ref[0]

    def clear(i, _):
        out_ref[pl.ds(pl.multiple_of(i * 16, 16), 16)] = jnp.zeros((16, 8, 128), F32)
        return 0

    lax.fori_loop(0, out_ref.shape[0] // 16, clear, 0)
    carry = jnp.zeros((128, 128), F32)
    for r in range(7):
        entering = carry * all_ref[r, 0:1, 50:51] + pltpu.roll(all_ref[r], 96, 1)
        entering = entering + all_ref[r, 0:1, 48:49] * all_ref[r + 1]
        if r > 0:
            entering = entering + all_ref[r, 0:1, 49:50] * pltpu.roll(all_ref[r - 1], 112, 1)
        carry = jnp.where(r < rank, entering, carry)
    right = jnp.where(rank < 7, all_ref[jnp.minimum(rank + 1, 7)], 0.0)
    left = pltpu.roll(all_ref[jnp.maximum(rank - 1, 0)], 112, 1)
    d_right, c_right, c_left, gain = (row_ref[i : i + 1, :] for i in range(4))
    spread = lambda value, k: jnp.broadcast_to(value[:, k : k + 1], (128, 128))
    top = lax.broadcasted_iota(jnp.int32, (8, 128), 0) < 4
    for k in range(16):
        g = g_ref[k]
        right_k = spread(right, k)
        detail = dz_ref[k] + g * plane_ref[:, 0:128] + right_k * d_right
        coarse = cz_ref[k] + g * plane_ref[:, 128:256] + right_k * c_right
        coarse = coarse + spread(left, k) * c_left + spread(carry, k) * gain
        detail_ref[k] = detail
        for i in range(16):
            c8, d8 = coarse[8 * i : 8 * i + 8], detail[8 * i : 8 * i + 8]
            block = 32 * k + 2 * i
            out_ref[place_ref[block]] = jnp.where(top, c8, pltpu.roll(d8, 4, 0))
            out_ref[place_ref[block + 1]] = jnp.where(top, pltpu.roll(c8, 4, 0), d8)


def shift(value, axis, by):
    count = lax.axis_size(axis)
    return lax.ppermute(value, axis, [(i, i + by) for i in range(count) if 0 <= i + by < count])


def local(
    nodal_field, spacing_x, spacing_z, operator_x, persist_x, operator_z, persist_z, receivers
):
    rank_x = lax.axis_index("gx").astype(jnp.int32).reshape(1)
    rank_z = lax.axis_index("gz").astype(jnp.int32).reshape(1)
    plane = jax.ShapeDtypeStruct((128, 256), F32)
    s, v = spec(SMEM), spec(VMEM)

    first, last = pl.pallas_call(
        edge_kernel,
        grid=(1,),
        in_specs=[
            s, s,
            pl.BlockSpec((2, 128, 256), lambda i: (0, 0, 0)),
            pl.BlockSpec((2, 128, 256), lambda i: (15, 0, 0)),
        ],
        out_specs=[pl.BlockSpec((128, 256), lambda i: (0, 0))] * 2,
        out_shape=[plane, plane],
        name="edge",
    )(rank_x, spacing_x, nodal_field, nodal_field)
    left = shift(last, "gx", 1)
    right = shift(first, "gx", -1)

    own = pl.pallas_call(
        tail_kernel,
        grid=(4,),
        in_specs=[s, s, s, pl.BlockSpec((32, 32, 256), lambda i: (0, i, 0))],
        out_specs=pl.BlockSpec((32, 256), lambda i: (i, 0)),
        out_shape=plane,
        cost_estimate=cost(64 * 32768, 4 << 20),
        name="tail",
    )(rank_x, spacing_x, operator_x, nodal_field)

    ended = pl.pallas_call(
        close_kernel,
        in_specs=[s, s, s, s, v, v, v],
        out_specs=v,
        out_shape=jax.ShapeDtypeStruct((136, 256), F32),
        name="close",
    )(rank_x, spacing_x, operator_x, persist_x, own, right, left)
    one, two, three = (shift(ended, "gx", by) for by in (1, 2, 3))

    near_space = lax.dynamic_slice_in_dim(spacing_z, rank_z[0] * 256, 256)
    high, low, rows = pl.pallas_call(
        table_kernel,
        in_specs=[s, s, v, v, v, v],
        out_specs=[v, v, v],
        out_shape=[
            jax.ShapeDtypeStruct((256, 256), BF16),
            jax.ShapeDtypeStruct((256, 256), BF16),
            jax.ShapeDtypeStruct((8, 128), F32),
        ],
        compiler_params=params(),
        cost_estimate=cost(6 * 256 * 256 * 128, 1 << 20),
        name="table",
    )(
        rank_z, spacing_z, near_space[0::2].reshape(1, 128), near_space[1::2].reshape(1, 128),
        operator_z, persist_z.reshape(1, 128),
    )

    chunk = 32
    whole = lambda shape: pl.BlockSpec(shape, lambda i: (0,) * len(shape))
    third = pl.BlockSpec((16, chunk, 128), lambda i: (0, i, 0))
    detail_x, dz, cz, columns = pl.pallas_call(
        main_kernel,
        grid=(128 // chunk,),
        in_specs=[
            s, s, s,
            pl.BlockSpec((32, chunk, 256), lambda i: (0, i, 0)),
            pl.BlockSpec((chunk, 256), lambda i: (i, 0)),
            pl.BlockSpec((chunk, 256), lambda i: (i, 0)),
            whole((256, 256)), whole((256, 256)),
        ],
        out_specs=[
            pl.BlockSpec((16, chunk, 256), lambda i: (0, i, 0)),
            third, third,
            pl.BlockSpec((chunk, 128), lambda i: (i, 0)),
        ],
        out_shape=[
            jax.ShapeDtypeStruct((16, 128, 256), F32),
            jax.ShapeDtypeStruct((16, 128, 128), F32),
            jax.ShapeDtypeStruct((16, 128, 128), F32),
            jax.ShapeDtypeStruct((128, 128), F32),
        ],
        scratch_shapes=[VMEM((4, 17, 8, 128), F32), VMEM((16, chunk, 256), F32)],
        compiler_params=params(),
        cost_estimate=cost(6 * 2048 * 256 * 256, 10 << 20),
        name="main",
    )(rank_x, spacing_x, operator_x, nodal_field, right, left, high, low)

    plane_pass, message = pl.pallas_call(
        carry_kernel,
        in_specs=[s, v, v, v, v, v, v, v],
        out_specs=[v, v],
        out_shape=[plane, jax.ShapeDtypeStruct((128, 128), F32)],
        compiler_params=params(),
        name="carry",
    )(persist_x, one, two, three, high, low, rows, columns)
    gathered = lax.all_gather(message, "gz")

    group = lax.axis_size("gy") * lax.axis_size("gz")
    capacity = 16
    targets = receivers[:, 0]
    positions = jnp.arange(512, dtype=jnp.int32)
    earlier = (targets[None, :] == targets[:, None]) & (positions[None, :] < positions[:, None])
    placed = targets * capacity + jnp.sum(earlier.astype(jnp.int32), axis=1)

    detail_z, outgoing = pl.pallas_call(
        last_kernel,
        in_specs=[s, s, s, v, v, v, v, v],
        out_specs=[v, v],
        out_shape=[
            jax.ShapeDtypeStruct((16, 128, 128), F32),
            jax.ShapeDtypeStruct((group * capacity, 8, 128), F32),
        ],
        compiler_params=params(),
        name="last",
    )(rank_z, persist_x, placed, dz, cz, plane_pass, gathered, rows)
    incoming = lax.all_to_all(
        outgoing.reshape(group, capacity, 8, 128), ("gy", "gz"), split_axis=0, concat_axis=0, tiled=True
    )
    received = incoming.reshape(1, group, capacity, 2, LINES, 128)
    return (detail_x, detail_z, received)


def solution(mesh):
    return jax.shard_map(
        local,
        mesh=mesh,
        in_specs=(
            P("gx", "gy", "gz"),
            P(),
            P(),
            P("gx", None),
            P("gx"),
            P("gz", None),
            P("gz"),
            P(("gx", "gy", "gz"), None),
        ),
        out_specs=(
            P("gx", "gy", "gz"),
            P("gx", "gy", "gz"),
            P(("gx", "gy", "gz"), None, None, None, None, None),
        ),
        check_vma=False,
    )
```

```python
import jax
import jax.numpy as jnp
from jax import lax
from jax.experimental import pallas as pl
from jax.experimental.pallas import tpu as pltpu
from jax.sharding import PartitionSpec as P

LINES = 4
F32 = jnp.float32
BF16 = jnp.bfloat16
SMEM = pltpu.SMEM
VMEM = pltpu.VMEM


def spec(space):
    return pl.BlockSpec(memory_space=space)


def cost(flops, moved):
    return pl.CostEstimate(flops=flops, bytes_accessed=moved, transcendentals=0)


def params(mib=16):
    return pltpu.CompilerParams(vmem_limit_bytes=mib << 20)


def weights_x(rank_ref, h_ref):
    own = pltpu.roll(jnp.broadcast_to(h_ref[...], (8, 128)), 128 - 32 * rank_ref[0], 1)
    after = pltpu.roll(own, 127, 1)
    total = own + after
    return after / total, own / total, 0.5 * own, 0.5 * after


def head_kernel(rank_ref, f_ref, h_ref, x_ref, first_ref, last_ref, out_ref):
    rows_of = weights_x(rank_ref, h_ref)
    weight = lambda i, k: rows_of[i][0:1, (2 * k) % 128 : (2 * k) % 128 + 1]
    far_before = jnp.where(rank_ref[0] > 0, weight(3, -1), 0.0)
    before = -f_ref[15, 0] * far_before * weight(1, -1)
    total = None
    for j in range(16):
        v = f_ref[15, j] * weight(2, j)
        if j < 15:
            v = v + f_ref[15, j + 1] * weight(3, j)
        term = (before - v * weight(0, j)) * x_ref[2 * j] + v * x_ref[2 * j + 1]
        total = term if total is None else total + term
        before = -v * weight(1, j)
    out_ref[...] = total
    first_ref[...] = x_ref[0]
    last_ref[...] = x_ref[31] - weight(0, 15) * x_ref[30]


def close_kernel(g_ref, row_ref, own_ref, right_ref, left_ref, out_ref):
    total = own_ref[...] + row_ref[15:16, 0:1] * right_ref[...] + row_ref[31:32, 0:1] * left_ref[...]
    out_ref[0:128, :] = total
    out_ref[128:136, :] = jnp.full((8, 256), g_ref[15], F32)


def split(value):
    high = value.astype(BF16)
    return high, (value - high.astype(F32)).astype(BF16)


def dot3(value, high, low):
    v_high, v_low = split(value)
    one = lambda a, b: jnp.dot(a, b, preferred_element_type=F32)
    return one(v_high, high) + (one(v_low, high) + one(v_high, low))


def dot_nt(a, b):
    return lax.dot_general(
        a, b, (((1,), (1,)), ((), ())), precision=lax.Precision.HIGHEST, preferred_element_type=F32
    )


def pass_matrix(even, odd, far_before, b_before, factor, nodes):
    total = even + odd
    a, b = odd / total, even / total
    near, far = 0.5 * even, 0.5 * odd
    z = lax.broadcasted_iota(jnp.int32, (nodes, 128), 0)
    k = lax.broadcasted_iota(jnp.int32, (nodes, 128), 1)
    chosen = jnp.where(z == 2 * k, 1.0, 0.0)
    detail = jnp.where(z == 2 * k + 1, 1.0, 0.0) - chosen * a - jnp.where(z == 2 * k + 2, b, 0.0)
    shifted = jnp.where(k == 0, 0.0, pltpu.roll(detail * far, 1, 1))
    load = detail * near + shifted
    load = load - jnp.where((z == 0) & (k == 0), far_before * b_before, 0.0)
    half = nodes // 2
    return detail, chosen[:, 0:half] + dot_nt(load[:, 0:half], factor), near, b


def table_kernel(
    rank_ref, rank_x_ref, h_ref, even_ref, odd_ref, f_ref, g_ref, hx_ref, fx_ref,
    high_ref, low_ref, row_ref, x_high_ref, x_low_ref, x_row_ref,
):
    at = jnp.maximum(rank_ref[0] * 256 - 2, 0)
    one = lambda value: jnp.full((1, 1), value, F32)
    h_even, h_odd = one(h_ref[at]), one(h_ref[at + 1])
    far_before = jnp.where(rank_ref[0] > 0, 0.5 * h_odd, 0.0)
    detail, coarse, near, b = pass_matrix(
        even_ref[...], odd_ref[...], far_before, h_even / (h_even + h_odd), f_ref[...], 256
    )
    high, low = split(detail)
    high_ref[:, 0:128], low_ref[:, 0:128] = high, low
    high, low = split(coarse)
    high_ref[:, 128:256], low_ref[:, 128:256] = high, low
    row = lax.broadcasted_iota(jnp.int32, (8, 128), 0)
    lane = lax.broadcasted_iota(jnp.int32, (8, 128), 1)
    pick = jnp.where(((row == 1) & (lane == 127)) | ((row == 2) & (lane == 0)), 1.0, 0.0)
    columns = dot_nt(pick, f_ref[...])
    last = lane[0:1] == 127
    from_right = columns[1:2] * (-near[:, 127:128] * b[:, 127:128])
    from_left = columns[2:3] * far_before
    gain = g_ref[...]
    row_ref[0:1] = jnp.where(last, -b, 0.0)
    row_ref[1:2] = from_right
    row_ref[2:3] = from_left
    row_ref[3:4] = gain
    row_ref[4:5] = jnp.broadcast_to(from_right[:, 127:128], (1, 128))
    row_ref[5:6] = jnp.broadcast_to(from_left[:, 127:128], (1, 128))
    row_ref[6:7] = jnp.broadcast_to(gain[:, 127:128], (1, 128))
    row_ref[7:8] = jnp.zeros((1, 128), F32)

    base = rank_x_ref[0] * 32
    node = lax.broadcasted_iota(jnp.int32, (128, 128), 0)
    place = lax.broadcasted_iota(jnp.int32, (128, 128), 1)
    index = jnp.where(place == 127, jnp.maximum(base - 2, 0), base + 2 * jnp.minimum(place, 15))
    h = jnp.broadcast_to(hx_ref[...], (8, 128))
    take = lambda where: jnp.dot(
        h, jnp.where(node == where, 1.0, 0.0), precision=lax.Precision.HIGHEST, preferred_element_type=F32
    )[0:1]
    even, odd = take(index), take(index + 1)
    far_before = jnp.where(rank_x_ref[0] > 0, 0.5 * odd[:, 127:128], 0.0)
    b_before = even[:, 127:128] / (even[:, 127:128] + odd[:, 127:128])
    factor = fx_ref[...]
    _, coarse, near, b = pass_matrix(even, odd, far_before, b_before, factor, 32)
    one_of = lambda n, m: jnp.where(
        lax.broadcasted_iota(jnp.int32, (n, m), 0) // 8 == lax.broadcasted_iota(jnp.int32, (n, m), 1), 1.0, 0.0
    )
    tall = jnp.dot(
        one_of(256, 32), coarse, precision=lax.Precision.HIGHEST, preferred_element_type=F32
    )
    both = dot_nt(one_of(128, 16), tall)
    same = (
        lax.broadcasted_iota(jnp.int32, (128, 256), 0) % 8
        == lax.broadcasted_iota(jnp.int32, (128, 256), 1) % 8
    )
    high, low = split(jnp.where(same, both, 0.0))
    x_high_ref[...], x_low_ref[...] = high, low
    x_row_ref[0:16, :] = jnp.broadcast_to(factor[:, 15:16] * (-near[:, 15:16] * b[:, 15:16]), (16, 128))
    x_row_ref[16:32, :] = jnp.broadcast_to(factor[:, 0:1] * far_before, (16, 128))


def dot3_left(high, low, value):
    v_high, v_low = split(value)
    one = lambda a, b: jnp.dot(a, b, preferred_element_type=F32)
    return one(high, v_high) + (one(high, v_low) + one(low, v_high))


def main_kernel(
    x_row_ref, x_ref, right_ref, left_ref, x_high_ref, x_low_ref, high_ref, low_ref,
    dz_ref, cz_ref, column_ref, v_ref,
):
    chunk = x_ref.shape[1]
    for step in range(chunk // 8):
        rows = slice(step * 8, step * 8 + 8)
        nodes = x_ref[:, rows, :].reshape(256, 256)
        coarse = dot3_left(x_high_ref[...], x_low_ref[...], nodes)
        for k in range(16):
            v_ref[k, rows, :] = (
                coarse[8 * k : 8 * k + 8]
                + x_row_ref[k : k + 1, 0:1] * right_ref[rows, :]
                + x_row_ref[16 + k : 17 + k, 0:1] * left_ref[rows, :]
            )
    values = v_ref[...].reshape(16 * chunk, 256)
    both = dot3(values, high_ref[...], low_ref[...])
    both = both.reshape(16, chunk, 256)
    dz_ref[...] = both[:, :, 0:128]
    cz_ref[...] = both[:, :, 128:256]
    lane = lax.broadcasted_iota(jnp.int32, (chunk, 128), 1)
    message = jnp.zeros((chunk, 128), F32)
    spread = lambda column: jnp.broadcast_to(column, (chunk, 128))
    for k in range(16):
        message = jnp.where(lane == k, spread(v_ref[k, :, 0:1]), message)
        message = jnp.where(lane == 16 + k, spread(dz_ref[k, :, 127:128]), message)
        tail = cz_ref[k, :, 127:128] - v_ref[k, :, 254:255]
        message = jnp.where(lane == 32 + k, spread(tail), message)
    column_ref[...] = message


def output_kernel(
    rank_ref, rank_x_ref, g_ref, h_ref, x_ref, right_ref, dz_ref, plane_ref, all_ref, row_ref,
    detail_x_ref, detail_z_ref,
):
    rows_of = weights_x(rank_x_ref, h_ref)
    weight = lambda i, k: rows_of[i][0:1, 2 * k : 2 * k + 1]
    for j in range(16):
        after = x_ref[2 * j + 2] if j < 15 else right_ref[...]
        detail_x_ref[j] = x_ref[2 * j + 1] - weight(0, j) * x_ref[2 * j] - weight(1, j) * after
    rank = rank_ref[0]
    chunk = x_ref.shape[1]
    rows = pl.ds(pl.multiple_of(pl.program_id(0) * chunk, chunk), chunk)
    edge = jnp.where(rank < 7, all_ref[jnp.minimum(rank + 1, 7), rows, :], 0.0)
    for k in range(16):
        spread = jnp.broadcast_to(edge[:, k : k + 1], (chunk, 128))
        detail_z_ref[k] = dz_ref[k] + g_ref[k] * plane_ref[:, 0:128] + spread * row_ref[0:1, :]


def carry_kernel(g_ref, one_ref, two_ref, three_ref, high_ref, low_ref, row_ref, column_ref, plane_ref, out_ref):
    carry = two_ref[0:128, :] + two_ref[128:129, :] * three_ref[0:128, :]
    carry = one_ref[0:128, :] + one_ref[128:129, :] * carry
    plane = dot3(carry, high_ref[...], low_ref[...])
    plane_ref[...] = plane
    lane = lax.broadcasted_iota(jnp.int32, (1, 128), 1)
    gain = jnp.zeros((1, 128), F32)
    for k in range(48):
        gain = jnp.where(lane == k, g_ref[k % 16], gain)
    spread = lambda column: jnp.broadcast_to(column, (128, 128))
    wide = lax.broadcasted_iota(jnp.int32, (128, 128), 1)
    pieces = jnp.where(
        wide < 16,
        spread(carry[:, 0:1]),
        jnp.where(wide < 32, spread(plane[:, 127:128]), spread(plane[:, 255:256] - carry[:, 254:255])),
    )
    message = column_ref[...] + gain * pieces
    for i in range(3):
        message = jnp.where(wide == 48 + i, row_ref[4 + i : 5 + i, :], message)
    out_ref[...] = message


def last_kernel(
    rank_ref, g_ref, place_ref, dz_ref, cz_ref, plane_ref, all_ref, row_ref, out_ref
):
    rank = rank_ref[0]

    def clear(i, _):
        out_ref[pl.ds(pl.multiple_of(i * 16, 16), 16)] = jnp.zeros((16, 8, 128), F32)
        return 0

    lax.fori_loop(0, out_ref.shape[0] // 16, clear, 0)
    carry = jnp.zeros((128, 128), F32)
    for r in range(7):
        entering = carry * all_ref[r, 0:1, 50:51] + pltpu.roll(all_ref[r], 96, 1)
        entering = entering + all_ref[r, 0:1, 48:49] * all_ref[r + 1]
        if r > 0:
            entering = entering + all_ref[r, 0:1, 49:50] * pltpu.roll(all_ref[r - 1], 112, 1)
        carry = jnp.where(r < rank, entering, carry)
    right = jnp.where(rank < 7, all_ref[jnp.minimum(rank + 1, 7)], 0.0)
    left = pltpu.roll(all_ref[jnp.maximum(rank - 1, 0)], 112, 1)
    d_right, c_right, c_left, gain = (row_ref[i : i + 1, :] for i in range(4))
    spread = lambda value, k: jnp.broadcast_to(value[:, k : k + 1], (128, 128))
    top = lax.broadcasted_iota(jnp.int32, (8, 128), 0) < 4
    for k in range(16):
        g = g_ref[k]
        right_k = spread(right, k)
        detail = dz_ref[k] + g * plane_ref[:, 0:128] + right_k * d_right
        coarse = cz_ref[k] + g * plane_ref[:, 128:256] + right_k * c_right
        coarse = coarse + spread(left, k) * c_left + spread(carry, k) * gain
        for i in range(16):
            c8, d8 = coarse[8 * i : 8 * i + 8], detail[8 * i : 8 * i + 8]
            block = 32 * k + 2 * i
            out_ref[place_ref[block]] = jnp.where(top, c8, pltpu.roll(d8, 4, 0))
            out_ref[place_ref[block + 1]] = jnp.where(top, pltpu.roll(c8, 4, 0), d8)


def shift(value, axis, by):
    count = lax.axis_size(axis)
    return lax.ppermute(value, axis, [(i, i + by) for i in range(count) if 0 <= i + by < count])


def local(
    nodal_field, spacing_x, spacing_z, operator_x, persist_x, operator_z, persist_z, receivers
):
    rank_x = lax.axis_index("gx").astype(jnp.int32).reshape(1)
    rank_z = lax.axis_index("gz").astype(jnp.int32).reshape(1)
    plane = jax.ShapeDtypeStruct((128, 256), F32)
    s, v = spec(SMEM), spec(VMEM)

    chunk = 32
    whole = lambda shape: pl.BlockSpec(shape, lambda i: (0,) * len(shape))
    nodes = pl.BlockSpec((32, chunk, 256), lambda i: (0, i, 0))
    thin = pl.BlockSpec((chunk, 256), lambda i: (i, 0))
    third = pl.BlockSpec((16, chunk, 128), lambda i: (0, i, 0))
    grid = (128 // chunk,)
    space_x = spacing_x.reshape(1, 128)

    first, last, own = pl.pallas_call(
        head_kernel,
        grid=grid,
        in_specs=[s, s, whole((1, 128)), nodes],
        out_specs=[thin, thin, thin],
        out_shape=[plane, plane, plane],
        cost_estimate=cost(64 * 32768, 4 << 20),
        name="head",
    )(rank_x, operator_x, space_x, nodal_field)
    left = shift(last, "gx", 1)
    right = shift(first, "gx", -1)

    near_space = lax.dynamic_slice_in_dim(spacing_z, rank_z[0] * 256, 256)
    square = jax.ShapeDtypeStruct((256, 256), BF16)
    oblong = jax.ShapeDtypeStruct((128, 256), BF16)
    high, low, rows, x_high, x_low, x_rows = pl.pallas_call(
        table_kernel,
        in_specs=[s, s, s, v, v, v, v, v, v],
        out_specs=[v] * 6,
        out_shape=[
            square, square, jax.ShapeDtypeStruct((8, 128), F32),
            oblong, oblong, jax.ShapeDtypeStruct((32, 128), F32),
        ],
        compiler_params=params(),
        cost_estimate=cost(12 * 256 * 256 * 128, 1 << 20),
        name="table",
    )(
        rank_z, rank_x, spacing_z, near_space[0::2].reshape(1, 128), near_space[1::2].reshape(1, 128),
        operator_z, persist_z.reshape(1, 128), space_x, operator_x,
    )

    ended = pl.pallas_call(
        close_kernel,
        in_specs=[s, v, v, v, v],
        out_specs=v,
        out_shape=jax.ShapeDtypeStruct((136, 256), F32),
        name="close",
    )(persist_x, x_rows, own, right, left)
    one, two, three = (shift(ended, "gx", by) for by in (1, 2, 3))

    dz, cz, columns = pl.pallas_call(
        main_kernel,
        grid=grid,
        in_specs=[
            whole((32, 128)), nodes, thin, thin,
            whole((128, 256)), whole((128, 256)), whole((256, 256)), whole((256, 256)),
        ],
        out_specs=[third, third, pl.BlockSpec((chunk, 128), lambda i: (i, 0))],
        out_shape=[
            jax.ShapeDtypeStruct((16, 128, 128), F32),
            jax.ShapeDtypeStruct((16, 128, 128), F32),
            jax.ShapeDtypeStruct((128, 128), F32),
        ],
        scratch_shapes=[VMEM((16, chunk, 256), F32)],
        compiler_params=params(),
        cost_estimate=cost(6 * 2048 * 256 * 256, 10 << 20),
        name="main",
    )(x_rows, nodal_field, right, left, x_high, x_low, high, low)

    plane_pass, message = pl.pallas_call(
        carry_kernel,
        in_specs=[s, v, v, v, v, v, v, v],
        out_specs=[v, v],
        out_shape=[plane, jax.ShapeDtypeStruct((128, 128), F32)],
        compiler_params=params(),
        name="carry",
    )(persist_x, one, two, three, high, low, rows, columns)
    gathered = lax.all_gather(message, "gz")

    group = lax.axis_size("gy") * lax.axis_size("gz")
    capacity = 16
    targets = receivers[:, 0]
    positions = jnp.arange(512, dtype=jnp.int32)
    earlier = (targets[None, :] == targets[:, None]) & (positions[None, :] < positions[:, None])
    placed = targets * capacity + jnp.sum(earlier.astype(jnp.int32), axis=1)

    outgoing = pl.pallas_call(
        last_kernel,
        in_specs=[s, s, s, v, v, v, v, v],
        out_specs=v,
        out_shape=jax.ShapeDtypeStruct((group * capacity, 8, 128), F32),
        compiler_params=params(),
        name="last",
    )(rank_z, persist_x, placed, dz, cz, plane_pass, gathered, rows)
    incoming = lax.all_to_all(
        outgoing.reshape(group, capacity, 8, 128), ("gy", "gz"), split_axis=0, concat_axis=0, tiled=True
    )
    detail_x, detail_z = pl.pallas_call(
        output_kernel,
        grid=grid,
        in_specs=[
            s, s, s, whole((1, 128)), nodes, thin, third, thin, whole((8, 128, 128)), whole((8, 128)),
        ],
        out_specs=[pl.BlockSpec((16, chunk, 256), lambda i: (0, i, 0)), third],
        out_shape=[
            jax.ShapeDtypeStruct((16, 128, 256), F32),
            jax.ShapeDtypeStruct((16, 128, 128), F32),
        ],
        compiler_params=params(),
        cost_estimate=cost(1 << 20, 8 << 20),
        name="output",
    )(rank_z, rank_x, persist_x, space_x, nodal_field, right, dz, plane_pass, gathered, rows)
    received = incoming.reshape(1, group, capacity, 2, LINES, 128)
    return (detail_x, detail_z, received)


def solution(mesh):
    return jax.shard_map(
        local,
        mesh=mesh,
        in_specs=(
            P("gx", "gy", "gz"),
            P(),
            P(),
            P("gx", None),
            P("gx"),
            P("gz", None),
            P("gz"),
            P(("gx", "gy", "gz"), None),
        ),
        out_specs=(
            P("gx", "gy", "gz"),
            P("gx", "gy", "gz"),
            P(("gx", "gy", "gz"), None, None, None, None, None),
        ),
        check_vma=False,
    )
```

```python
import jax
import jax.numpy as jnp
from jax import lax
from jax.experimental import pallas as pl
from jax.experimental.pallas import tpu as pltpu
from jax.sharding import PartitionSpec as P

LINES = 4
F32 = jnp.float32
BF16 = jnp.bfloat16
SMEM = pltpu.SMEM
VMEM = pltpu.VMEM


def spec(space):
    return pl.BlockSpec(memory_space=space)


def cost(flops, moved):
    return pl.CostEstimate(flops=flops, bytes_accessed=moved, transcendentals=0)


def params(mib=56):
    return pltpu.CompilerParams(vmem_limit_bytes=mib << 20)


def weights_x(rank_ref, h_ref):
    own = pltpu.roll(jnp.broadcast_to(h_ref[...], (8, 128)), 128 - 32 * rank_ref[0], 1)
    after = pltpu.roll(own, 127, 1)
    total = own + after
    return after / total, own / total, 0.5 * own, 0.5 * after


def head_kernel(rank_ref, f_ref, h_ref, x_ref, first_ref, last_ref, out_ref, w_ref):
    @pl.when(pl.program_id(0) == 0)
    def _():
        rows_of = weights_x(rank_ref, h_ref)
        weight = lambda i, k: jnp.broadcast_to(rows_of[i][:, (2 * k) % 128 : (2 * k) % 128 + 1], (8, 128))
        far_before = jnp.where(rank_ref[0] > 0, weight(3, -1), 0.0)
        before = -f_ref[15, 0] * far_before * weight(1, -1)
        for j in range(16):
            v = f_ref[15, j] * weight(2, j)
            if j < 15:
                v = v + f_ref[15, j + 1] * weight(3, j)
            w_ref[2 * j] = before - v * weight(0, j)
            w_ref[2 * j + 1] = v
            before = -v * weight(1, j)
        w_ref[32] = weight(0, 15)

    for r in range(x_ref.shape[1] // 8):
        for half in range(2):
            at = (slice(8 * r, 8 * r + 8), slice(128 * half, 128 * half + 128))
            total = w_ref[0] * x_ref[(0, *at)]
            for x in range(1, 32):
                total = total + w_ref[x] * x_ref[(x, *at)]
            out_ref[at] = total
            first_ref[at] = x_ref[(0, *at)]
            last_ref[at] = x_ref[(31, *at)] - w_ref[32] * x_ref[(30, *at)]


def close_kernel(g_ref, row_ref, own_ref, right_ref, left_ref, out_ref):
    total = own_ref[...] + row_ref[15:16, 0:1] * right_ref[...] + row_ref[31:32, 0:1] * left_ref[...]
    out_ref[0:128, :] = total
    out_ref[128:136, :] = jnp.full((8, 256), g_ref[15], F32)


def split(value):
    high = value.astype(BF16)
    return high, (value - high.astype(F32)).astype(BF16)


def dot3(value, high, low):
    v_high, v_low = split(value)
    one = lambda a, b: jnp.dot(a, b, preferred_element_type=F32)
    return one(v_high, high) + (one(v_low, high) + one(v_high, low))


def dot_nt(a, b):
    return lax.dot_general(
        a, b, (((1,), (1,)), ((), ())), precision=lax.Precision.HIGHEST, preferred_element_type=F32
    )


def pass_matrix(even, odd, far_before, b_before, factor, nodes):
    total = even + odd
    a, b = odd / total, even / total
    near, far = 0.5 * even, 0.5 * odd
    z = lax.broadcasted_iota(jnp.int32, (nodes, 128), 0)
    k = lax.broadcasted_iota(jnp.int32, (nodes, 128), 1)
    chosen = jnp.where(z == 2 * k, 1.0, 0.0)
    detail = jnp.where(z == 2 * k + 1, 1.0, 0.0) - chosen * a - jnp.where(z == 2 * k + 2, b, 0.0)
    shifted = jnp.where(k == 0, 0.0, pltpu.roll(detail * far, 1, 1))
    load = detail * near + shifted
    load = load - jnp.where((z == 0) & (k == 0), far_before * b_before, 0.0)
    half = nodes // 2
    return detail, chosen[:, 0:half] + dot_nt(load[:, 0:half], factor), near, b


def table_kernel(
    rank_ref, rank_x_ref, h_ref, even_ref, odd_ref, f_ref, g_ref, hx_ref, fx_ref,
    high_ref, low_ref, row_ref, x_high_ref, x_low_ref, x_row_ref,
):
    at = jnp.maximum(rank_ref[0] * 256 - 2, 0)
    one = lambda value: jnp.full((1, 1), value, F32)
    h_even, h_odd = one(h_ref[at]), one(h_ref[at + 1])
    far_before = jnp.where(rank_ref[0] > 0, 0.5 * h_odd, 0.0)
    detail, coarse, near, b = pass_matrix(
        even_ref[...], odd_ref[...], far_before, h_even / (h_even + h_odd), f_ref[...], 256
    )
    high, low = split(detail)
    high_ref[:, 0:128], low_ref[:, 0:128] = high, low
    high, low = split(coarse)
    high_ref[:, 128:256], low_ref[:, 128:256] = high, low
    row = lax.broadcasted_iota(jnp.int32, (8, 128), 0)
    lane = lax.broadcasted_iota(jnp.int32, (8, 128), 1)
    pick = jnp.where(((row == 1) & (lane == 127)) | ((row == 2) & (lane == 0)), 1.0, 0.0)
    columns = dot_nt(pick, f_ref[...])
    last = lane[0:1] == 127
    from_right = columns[1:2] * (-near[:, 127:128] * b[:, 127:128])
    from_left = columns[2:3] * far_before
    gain = g_ref[...]
    row_ref[0:1] = jnp.where(last, -b, 0.0)
    row_ref[1:2] = from_right
    row_ref[2:3] = from_left
    row_ref[3:4] = gain
    row_ref[4:5] = jnp.broadcast_to(from_right[:, 127:128], (1, 128))
    row_ref[5:6] = jnp.broadcast_to(from_left[:, 127:128], (1, 128))
    row_ref[6:7] = jnp.broadcast_to(gain[:, 127:128], (1, 128))
    row_ref[7:8] = jnp.zeros((1, 128), F32)

    base = rank_x_ref[0] * 32
    node = lax.broadcasted_iota(jnp.int32, (128, 128), 0)
    place = lax.broadcasted_iota(jnp.int32, (128, 128), 1)
    index = jnp.where(place == 127, jnp.maximum(base - 2, 0), base + 2 * jnp.minimum(place, 15))
    h = jnp.broadcast_to(hx_ref[...], (8, 128))
    take = lambda where: jnp.dot(
        h, jnp.where(node == where, 1.0, 0.0), precision=lax.Precision.HIGHEST, preferred_element_type=F32
    )[0:1]
    even, odd = take(index), take(index + 1)
    far_before = jnp.where(rank_x_ref[0] > 0, 0.5 * odd[:, 127:128], 0.0)
    b_before = even[:, 127:128] / (even[:, 127:128] + odd[:, 127:128])
    factor = fx_ref[...]
    _, coarse, near, b = pass_matrix(even, odd, far_before, b_before, factor, 32)
    one_of = lambda n, m: jnp.where(
        lax.broadcasted_iota(jnp.int32, (n, m), 0) // 8 == lax.broadcasted_iota(jnp.int32, (n, m), 1), 1.0, 0.0
    )
    tall = jnp.dot(
        one_of(256, 32), coarse, precision=lax.Precision.HIGHEST, preferred_element_type=F32
    )
    both = dot_nt(one_of(128, 16), tall)
    same = (
        lax.broadcasted_iota(jnp.int32, (128, 256), 0) % 8
        == lax.broadcasted_iota(jnp.int32, (128, 256), 1) % 8
    )
    high, low = split(jnp.where(same, both, 0.0))
    x_high_ref[...], x_low_ref[...] = high, low
    x_row_ref[0:16, :] = jnp.broadcast_to(factor[:, 15:16] * (-near[:, 15:16] * b[:, 15:16]), (16, 128))
    x_row_ref[16:32, :] = jnp.broadcast_to(factor[:, 0:1] * far_before, (16, 128))


def dot3_left(high, low, value):
    v_high, v_low = split(value)
    one = lambda a, b: jnp.dot(a, b, preferred_element_type=F32)
    return one(high, v_high) + (one(high, v_low) + one(low, v_high))


def main_kernel(
    x_row_ref, x_ref, right_ref, left_ref, x_high_ref, x_low_ref, high_ref, low_ref,
    dz_ref, cz_ref, column_ref, v_ref,
):
    chunk = x_ref.shape[1]
    for step in range(chunk // 8):
        rows = slice(step * 8, step * 8 + 8)
        nodes = x_ref[:, rows, :].reshape(256, 256)
        coarse = dot3_left(x_high_ref[...], x_low_ref[...], nodes)
        for k in range(16):
            v_ref[k, rows, :] = (
                coarse[8 * k : 8 * k + 8]
                + x_row_ref[k : k + 1, 0:1] * right_ref[rows, :]
                + x_row_ref[16 + k : 17 + k, 0:1] * left_ref[rows, :]
            )
    values = v_ref[...].reshape(16 * chunk, 256)
    both = dot3(values, high_ref[...], low_ref[...])
    both = both.reshape(16, chunk, 256)
    dz_ref[...] = both[:, :, 0:128]
    cz_ref[...] = both[:, :, 128:256]
    lane = lax.broadcasted_iota(jnp.int32, (chunk, 128), 1)
    message = jnp.zeros((chunk, 128), F32)
    spread = lambda column: jnp.broadcast_to(column, (chunk, 128))
    for k in range(16):
        message = jnp.where(lane == k, spread(v_ref[k, :, 0:1]), message)
        message = jnp.where(lane == 16 + k, spread(dz_ref[k, :, 127:128]), message)
        tail = cz_ref[k, :, 127:128] - v_ref[k, :, 254:255]
        message = jnp.where(lane == 32 + k, spread(tail), message)
    column_ref[...] = message


def output_kernel(
    rank_ref, rank_x_ref, g_ref, h_ref, x_ref, right_ref, dz_ref, plane_ref, all_ref, row_ref,
    detail_x_ref, detail_z_ref,
):
    rows_of = weights_x(rank_x_ref, h_ref)
    weight = lambda i, k: rows_of[i][0:1, 2 * k : 2 * k + 1]
    for j in range(16):
        after = x_ref[2 * j + 2] if j < 15 else right_ref[...]
        detail_x_ref[j] = x_ref[2 * j + 1] - weight(0, j) * x_ref[2 * j] - weight(1, j) * after
    rank = rank_ref[0]
    chunk = x_ref.shape[1]
    rows = pl.ds(pl.multiple_of(pl.program_id(0) * chunk, chunk), chunk)
    edge = jnp.where(rank < 7, all_ref[jnp.minimum(rank + 1, 7), rows, :], 0.0)
    for k in range(16):
        spread = jnp.broadcast_to(edge[:, k : k + 1], (chunk, 128))
        detail_z_ref[k] = dz_ref[k] + g_ref[k] * plane_ref[:, 0:128] + spread * row_ref[0:1, :]


def carry_kernel(g_ref, one_ref, two_ref, three_ref, high_ref, low_ref, row_ref, column_ref, plane_ref, out_ref):
    carry = two_ref[0:128, :] + two_ref[128:129, :] * three_ref[0:128, :]
    carry = one_ref[0:128, :] + one_ref[128:129, :] * carry
    plane = dot3(carry, high_ref[...], low_ref[...])
    plane_ref[...] = plane
    lane = lax.broadcasted_iota(jnp.int32, (1, 128), 1)
    gain = jnp.zeros((1, 128), F32)
    for k in range(48):
        gain = jnp.where(lane == k, g_ref[k % 16], gain)
    spread = lambda column: jnp.broadcast_to(column, (128, 128))
    wide = lax.broadcasted_iota(jnp.int32, (128, 128), 1)
    pieces = jnp.where(
        wide < 16,
        spread(carry[:, 0:1]),
        jnp.where(wide < 32, spread(plane[:, 127:128]), spread(plane[:, 255:256] - carry[:, 254:255])),
    )
    message = column_ref[...] + gain * pieces
    for i in range(3):
        message = jnp.where(wide == 48 + i, row_ref[4 + i : 5 + i, :], message)
    out_ref[...] = message


def place_kernel(g_ref, place_ref, dz_ref, cz_ref, plane_ref, message_ref, row_ref, out_ref, note_ref):
    note_ref[0:128] = message_ref[...]
    note_ref[128:136] = row_ref[...]

    def clear(i, _):
        out_ref[pl.ds(pl.multiple_of(i * 16, 16), 16)] = jnp.zeros((16, 8, 128), F32)
        return 0

    lax.fori_loop(0, out_ref.shape[0] // 16, clear, 0)
    top = lax.broadcasted_iota(jnp.int32, (8, 128), 0) < 4
    for k in range(16):
        g = g_ref[k]
        detail = dz_ref[k] + g * plane_ref[:, 0:128]
        coarse = cz_ref[k] + g * plane_ref[:, 128:256]
        for i in range(16):
            c8, d8 = coarse[8 * i : 8 * i + 8], detail[8 * i : 8 * i + 8]
            block = 32 * k + 2 * i
            out_ref[place_ref[block]] = jnp.where(top, c8, pltpu.roll(d8, 4, 0))
            out_ref[place_ref[block + 1]] = jnp.where(top, pltpu.roll(c8, 4, 0), d8)


def lines_kernel(rank_ref, rank_y_ref, place_ref, all_ref, out_ref, z_ref):
    rank = rank_ref[0]
    columns = lambda r: all_ref[r, 0:128, :]
    carry = jnp.zeros((128, 128), F32)
    for r in range(7):
        entering = carry * all_ref[r, 0:1, 50:51] + pltpu.roll(columns(r), 96, 1)
        entering = entering + all_ref[r, 0:1, 48:49] * columns(r + 1)
        if r > 0:
            entering = entering + all_ref[r, 0:1, 49:50] * pltpu.roll(columns(r - 1), 112, 1)
        carry = jnp.where(r < rank, entering, carry)
    right = jnp.where(rank < 7, columns(jnp.minimum(rank + 1, 7)), 0.0)
    left = columns(jnp.maximum(rank - 1, 0))
    wide = lax.broadcasted_iota(jnp.int32, (128, 128), 1)
    z_ref[...] = jnp.where(
        wide < 16, carry, jnp.where(wide < 32, pltpu.roll(right, 16, 1), pltpu.roll(left, 16, 1))
    )
    out_ref[...] = jnp.zeros(out_ref.shape, F32)
    lane = lax.broadcasted_iota(jnp.int32, (8, 128), 1)

    def body(pair, _):
        k, i = pair // 16, pair % 16
        piece = z_ref[pl.ds(pl.multiple_of(i * 8, 8), 8), :]
        for odd in range(2):
            place = place_ref[2 * pair + odd]
            to, slot = place // 16, place % 16
            ahead_y = (to // 8 - rank_y_ref[0] + 8) % 8
            ahead_z = (to % 8 - rank + 8) % 8
            moved = pltpu.roll(piece, (slot - k + 128) % 128, 1)
            mine = ((lane % 16) == slot) & (lane < 48)
            part = slice(4 * odd, 4 * odd + 4)
            out_ref[ahead_y, ahead_z] = jnp.where(mine[part], moved[part], out_ref[ahead_y, ahead_z])
        return 0

    lax.fori_loop(0, 256, body, 0)


def receive_kernel(rank_ref, rank_y_ref, tile_ref, line_ref, all_ref, out_ref):
    top = lax.broadcasted_iota(jnp.int32, (8, 128), 0) < 4
    for q in range(8):
        row = lambda i: jnp.broadcast_to(all_ref[q, 128 + i : 129 + i, :], (8, 128))
        of_carry = jnp.where(top, row(3), 0.0)
        of_right = jnp.where(top, row(1), row(0))
        of_left = jnp.where(top, row(2), 0.0)
        line = line_ref[(rank_ref[0] - q + 8) % 8, (rank_y_ref[0] - pl.program_id(0) + 8) % 8]
        lines = jnp.concatenate([line, line], axis=0)
        spread = lambda lane: jnp.broadcast_to(lines[:, lane : lane + 1], (8, 128))
        for m in range(16):
            t = 16 * q + m
            out_ref[t] = (
                tile_ref[t] + spread(m) * of_carry + spread(16 + m) * of_right + spread(32 + m) * of_left
            )


def shift(value, axis, by):
    count = lax.axis_size(axis)
    return lax.ppermute(value, axis, [(i, i + by) for i in range(count) if 0 <= i + by < count])


def ring(value, axis, by):
    count = lax.axis_size(axis)
    if by == 0:
        return value
    return lax.ppermute(value, axis, [(i, (i + by) % count) for i in range(count)])


def local(
    nodal_field, spacing_x, spacing_z, operator_x, persist_x, operator_z, persist_z, receivers
):
    rank_x = lax.axis_index("gx").astype(jnp.int32).reshape(1)
    rank_z = lax.axis_index("gz").astype(jnp.int32).reshape(1)
    rank_y = lax.axis_index("gy").astype(jnp.int32).reshape(1)
    plane = jax.ShapeDtypeStruct((128, 256), F32)
    s, v = spec(SMEM), spec(VMEM)

    chunk = 32
    whole = lambda shape: pl.BlockSpec(shape, lambda i: (0,) * len(shape))
    nodes = pl.BlockSpec((32, chunk, 256), lambda i: (0, i, 0))
    thin = pl.BlockSpec((chunk, 256), lambda i: (i, 0))
    third = pl.BlockSpec((16, chunk, 128), lambda i: (0, i, 0))
    grid = (128 // chunk,)
    space_x = spacing_x.reshape(1, 128)

    first, last, own = pl.pallas_call(
        head_kernel,
        grid=grid,
        in_specs=[s, s, whole((1, 128)), nodes],
        out_specs=[thin, thin, thin],
        out_shape=[plane, plane, plane],
        scratch_shapes=[VMEM((33, 8, 128), F32)],
        compiler_params=params(),
        cost_estimate=cost(64 * 32768, 4 << 20),
        name="head",
    )(rank_x, operator_x, space_x, nodal_field)
    left = shift(last, "gx", 1)
    right = shift(first, "gx", -1)

    near_space = lax.dynamic_slice_in_dim(spacing_z, rank_z[0] * 256, 256)
    square = jax.ShapeDtypeStruct((256, 256), BF16)
    oblong = jax.ShapeDtypeStruct((128, 256), BF16)
    high, low, rows, x_high, x_low, x_rows = pl.pallas_call(
        table_kernel,
        in_specs=[s, s, s, v, v, v, v, v, v],
        out_specs=[v] * 6,
        out_shape=[
            square, square, jax.ShapeDtypeStruct((8, 128), F32),
            oblong, oblong, jax.ShapeDtypeStruct((32, 128), F32),
        ],
        compiler_params=params(),
        cost_estimate=cost(12 * 256 * 256 * 128, 1 << 20),
        name="table",
    )(
        rank_z, rank_x, spacing_z, near_space[0::2].reshape(1, 128), near_space[1::2].reshape(1, 128),
        operator_z, persist_z.reshape(1, 128), space_x, operator_x,
    )

    ended = pl.pallas_call(
        close_kernel,
        in_specs=[s, v, v, v, v],
        out_specs=v,
        out_shape=jax.ShapeDtypeStruct((136, 256), F32),
        compiler_params=params(),
        name="close",
    )(persist_x, x_rows, own, right, left)
    one, two, three = (shift(ended, "gx", by) for by in (1, 2, 3))

    dz, cz, columns = pl.pallas_call(
        main_kernel,
        grid=grid,
        in_specs=[
            whole((32, 128)), nodes, thin, thin,
            whole((128, 256)), whole((128, 256)), whole((256, 256)), whole((256, 256)),
        ],
        out_specs=[third, third, pl.BlockSpec((chunk, 128), lambda i: (i, 0))],
        out_shape=[
            jax.ShapeDtypeStruct((16, 128, 128), F32),
            jax.ShapeDtypeStruct((16, 128, 128), F32),
            jax.ShapeDtypeStruct((128, 128), F32),
        ],
        scratch_shapes=[VMEM((16, chunk, 256), F32)],
        compiler_params=params(),
        cost_estimate=cost(6 * 2048 * 256 * 256, 10 << 20),
        name="main",
    )(x_rows, nodal_field, right, left, x_high, x_low, high, low)

    plane_pass, message = pl.pallas_call(
        carry_kernel,
        in_specs=[s, v, v, v, v, v, v, v],
        out_specs=[v, v],
        out_shape=[plane, jax.ShapeDtypeStruct((128, 128), F32)],
        compiler_params=params(),
        name="carry",
    )(persist_x, one, two, three, high, low, rows, columns)

    group = lax.axis_size("gy") * lax.axis_size("gz")
    capacity = 16
    targets = receivers[:, 0]
    positions = jnp.arange(512, dtype=jnp.int32)
    earlier = (targets[None, :] == targets[:, None]) & (positions[None, :] < positions[:, None])
    placed = targets * capacity + jnp.sum(earlier.astype(jnp.int32), axis=1)

    outgoing, note = pl.pallas_call(
        place_kernel,
        in_specs=[s, s, v, v, v, v, v],
        out_specs=[v, v],
        out_shape=[
            jax.ShapeDtypeStruct((group * capacity, 8, 128), F32),
            jax.ShapeDtypeStruct((136, 128), F32),
        ],
        compiler_params=params(),
        name="place",
    )(persist_x, placed, dz, cz, plane_pass, message, rows)
    incoming = lax.all_to_all(
        outgoing.reshape(group, capacity, 8, 128), ("gy", "gz"), split_axis=0, concat_axis=0, tiled=True
    )
    gathered = lax.all_gather(note, "gz")
    lines = pl.pallas_call(
        lines_kernel,
        in_specs=[s, s, s, v],
        out_specs=v,
        out_shape=jax.ShapeDtypeStruct((8, 8, 4, 128), F32),
        scratch_shapes=[VMEM((128, 128), F32)],
        compiler_params=params(),
        cost_estimate=cost(1 << 24, 1 << 20),
        name="lines",
    )(rank_z, rank_y, placed, gathered)
    moved = jnp.stack([ring(lines[by], "gy", by) for by in range(8)])
    lines_in = jnp.stack([ring(moved[:, by], "gz", by) for by in range(8)])
    detail_x, detail_z = pl.pallas_call(
        output_kernel,
        grid=grid,
        in_specs=[
            s, s, s, whole((1, 128)), nodes, thin, third, thin, whole((8, 136, 128)), whole((8, 128)),
        ],
        out_specs=[pl.BlockSpec((16, chunk, 256), lambda i: (0, i, 0)), third],
        out_shape=[
            jax.ShapeDtypeStruct((16, 128, 256), F32),
            jax.ShapeDtypeStruct((16, 128, 128), F32),
        ],
        compiler_params=params(),
        cost_estimate=cost(1 << 20, 8 << 20),
        name="output",
    )(rank_z, rank_x, persist_x, space_x, nodal_field, right, dz, plane_pass, gathered, rows)
    tiles = pl.BlockSpec((128, 8, 128), lambda i: (i, 0, 0))
    complete = pl.pallas_call(
        receive_kernel,
        grid=(group // 8,),
        in_specs=[s, s, tiles, whole((8, 8, 4, 128)), whole((8, 136, 128))],
        out_specs=tiles,
        out_shape=jax.ShapeDtypeStruct((group * capacity, 8, 128), F32),
        compiler_params=params(),
        name="receive",
    )(rank_z, rank_y, incoming.reshape(group * capacity, 8, 128), lines_in, gathered)
    received = complete.reshape(1, group, capacity, 2, LINES, 128)
    return (detail_x, detail_z, received)


def solution(mesh):
    return jax.shard_map(
        local,
        mesh=mesh,
        in_specs=(
            P("gx", "gy", "gz"),
            P(),
            P(),
            P("gx", None),
            P("gx"),
            P("gz", None),
            P("gz"),
            P(("gx", "gy", "gz"), None),
        ),
        out_specs=(
            P("gx", "gy", "gz"),
            P("gx", "gy", "gz"),
            P(("gx", "gy", "gz"), None, None, None, None, None),
        ),
        check_vma=False,
    )
```

```python
import jax
import jax.numpy as jnp
from jax import lax
from jax.experimental import pallas as pl
from jax.experimental.pallas import tpu as pltpu
from jax.sharding import PartitionSpec as P

LINES = 4
F32 = jnp.float32
BF16 = jnp.bfloat16
SMEM = pltpu.SMEM
VMEM = pltpu.VMEM


def spec(space):
    return pl.BlockSpec(memory_space=space)


def cost(flops, moved):
    return pl.CostEstimate(flops=flops, bytes_accessed=moved, transcendentals=0)


def params(mib=48):
    return pltpu.CompilerParams(vmem_limit_bytes=mib << 20)


def weights_x(rank_ref, h_ref):
    own = pltpu.roll(jnp.broadcast_to(h_ref[...], (8, 128)), 128 - 32 * rank_ref[0], 1)
    after = pltpu.roll(own, 127, 1)
    total = own + after
    return after / total, own / total, 0.5 * own, 0.5 * after


def head_kernel(rank_ref, f_ref, h_ref, x_ref, first_ref, last_ref, out_ref, w_ref):
    @pl.when(pl.program_id(0) == 0)
    def _():
        rows_of = weights_x(rank_ref, h_ref)
        weight = lambda i, k: jnp.broadcast_to(rows_of[i][:, (2 * k) % 128 : (2 * k) % 128 + 1], (8, 128))
        far_before = jnp.where(rank_ref[0] > 0, weight(3, -1), 0.0)
        before = -f_ref[15, 0] * far_before * weight(1, -1)
        for j in range(16):
            v = f_ref[15, j] * weight(2, j)
            if j < 15:
                v = v + f_ref[15, j + 1] * weight(3, j)
            w_ref[2 * j] = before - v * weight(0, j)
            w_ref[2 * j + 1] = v
            before = -v * weight(1, j)
        w_ref[32] = weight(0, 15)

    for r in range(x_ref.shape[1] // 8):
        for half in range(2):
            at = (slice(8 * r, 8 * r + 8), slice(128 * half, 128 * half + 128))
            total = w_ref[0] * x_ref[(0, *at)]
            for x in range(1, 32):
                total = total + w_ref[x] * x_ref[(x, *at)]
            out_ref[at] = total
            first_ref[at] = x_ref[(0, *at)]
            last_ref[at] = x_ref[(31, *at)] - w_ref[32] * x_ref[(30, *at)]


def close_kernel(g_ref, row_ref, own_ref, right_ref, left_ref, out_ref):
    total = own_ref[...] + row_ref[15:16, 0:1] * right_ref[...] + row_ref[31:32, 0:1] * left_ref[...]
    out_ref[0:128, :] = total
    out_ref[128:136, :] = jnp.full((8, 256), g_ref[15], F32)


def split(value):
    high = value.astype(BF16)
    return high, (value - high.astype(F32)).astype(BF16)


def dot3(value, high, low):
    v_high, v_low = split(value)
    one = lambda a, b: jnp.dot(a, b, preferred_element_type=F32)
    return one(v_high, high) + (one(v_low, high) + one(v_high, low))


def dot_nt(a, b):
    return lax.dot_general(
        a, b, (((1,), (1,)), ((), ())), precision=lax.Precision.HIGHEST, preferred_element_type=F32
    )


def pass_matrix(even, odd, far_before, b_before, factor, nodes):
    total = even + odd
    a, b = odd / total, even / total
    near, far = 0.5 * even, 0.5 * odd
    z = lax.broadcasted_iota(jnp.int32, (nodes, 128), 0)
    k = lax.broadcasted_iota(jnp.int32, (nodes, 128), 1)
    chosen = jnp.where(z == 2 * k, 1.0, 0.0)
    detail = jnp.where(z == 2 * k + 1, 1.0, 0.0) - chosen * a - jnp.where(z == 2 * k + 2, b, 0.0)
    shifted = jnp.where(k == 0, 0.0, pltpu.roll(detail * far, 1, 1))
    load = detail * near + shifted
    load = load - jnp.where((z == 0) & (k == 0), far_before * b_before, 0.0)
    half = nodes // 2
    return detail, chosen[:, 0:half] + dot_nt(load[:, 0:half], factor), near, b


def table_kernel(rank_ref, h_ref, even_ref, odd_ref, f_ref, g_ref, high_ref, low_ref, row_ref):
    at = jnp.maximum(rank_ref[0] * 256 - 2, 0)
    one = lambda value: jnp.full((1, 1), value, F32)
    h_even, h_odd = one(h_ref[at]), one(h_ref[at + 1])
    far_before = jnp.where(rank_ref[0] > 0, 0.5 * h_odd, 0.0)
    detail, coarse, near, b = pass_matrix(
        even_ref[...], odd_ref[...], far_before, h_even / (h_even + h_odd), f_ref[...], 256
    )
    high, low = split(detail)
    high_ref[:, 0:128], low_ref[:, 0:128] = high, low
    high, low = split(coarse)
    high_ref[:, 128:256], low_ref[:, 128:256] = high, low
    row = lax.broadcasted_iota(jnp.int32, (8, 128), 0)
    lane = lax.broadcasted_iota(jnp.int32, (8, 128), 1)
    pick = jnp.where(((row == 1) & (lane == 127)) | ((row == 2) & (lane == 0)), 1.0, 0.0)
    columns = dot_nt(pick, f_ref[...])
    last = lane[0:1] == 127
    from_right = columns[1:2] * (-near[:, 127:128] * b[:, 127:128])
    from_left = columns[2:3] * far_before
    gain = g_ref[...]
    row_ref[0:1] = jnp.where(last, -b, 0.0)
    row_ref[1:2] = from_right
    row_ref[2:3] = from_left
    row_ref[3:4] = gain
    row_ref[4:5] = jnp.broadcast_to(from_right[:, 127:128], (1, 128))
    row_ref[5:6] = jnp.broadcast_to(from_left[:, 127:128], (1, 128))
    row_ref[6:7] = jnp.broadcast_to(gain[:, 127:128], (1, 128))
    row_ref[7:8] = jnp.zeros((1, 128), F32)


def table_x_kernel(rank_x_ref, hx_ref, fx_ref, x_high_ref, x_low_ref, x_row_ref):
    base = rank_x_ref[0] * 32
    node = lax.broadcasted_iota(jnp.int32, (128, 128), 0)
    place = lax.broadcasted_iota(jnp.int32, (128, 128), 1)
    index = jnp.where(place == 127, jnp.maximum(base - 2, 0), base + 2 * jnp.minimum(place, 15))
    h = jnp.broadcast_to(hx_ref[...], (8, 128))
    take = lambda where: jnp.dot(
        h, jnp.where(node == where, 1.0, 0.0), precision=lax.Precision.HIGHEST, preferred_element_type=F32
    )[0:1]
    even, odd = take(index), take(index + 1)
    far_before = jnp.where(rank_x_ref[0] > 0, 0.5 * odd[:, 127:128], 0.0)
    b_before = even[:, 127:128] / (even[:, 127:128] + odd[:, 127:128])
    factor = fx_ref[...]
    _, coarse, near, b = pass_matrix(even, odd, far_before, b_before, factor, 32)
    one_of = lambda n, m: jnp.where(
        lax.broadcasted_iota(jnp.int32, (n, m), 0) // 8 == lax.broadcasted_iota(jnp.int32, (n, m), 1), 1.0, 0.0
    )
    tall = jnp.dot(
        one_of(256, 32), coarse, precision=lax.Precision.HIGHEST, preferred_element_type=F32
    )
    both = dot_nt(one_of(128, 16), tall)
    same = (
        lax.broadcasted_iota(jnp.int32, (128, 256), 0) % 8
        == lax.broadcasted_iota(jnp.int32, (128, 256), 1) % 8
    )
    high, low = split(jnp.where(same, both, 0.0))
    x_high_ref[...], x_low_ref[...] = high, low
    x_row_ref[0:16, :] = jnp.broadcast_to(factor[:, 15:16] * (-near[:, 15:16] * b[:, 15:16]), (16, 128))
    x_row_ref[16:32, :] = jnp.broadcast_to(factor[:, 0:1] * far_before, (16, 128))


def dot3_left(high, low, value):
    v_high, v_low = split(value)
    one = lambda a, b: jnp.dot(a, b, preferred_element_type=F32)
    return one(high, v_high) + (one(high, v_low) + one(low, v_high))


def main_kernel(
    rank_x_ref, h_ref, x_row_ref, x_ref, right_ref, left_ref, x_high_ref, x_low_ref, high_ref, low_ref,
    detail_x_ref, dz_ref, cz_ref, column_ref, v_ref, w_ref,
):
    @pl.when(pl.program_id(0) == 0)
    def _():
        rows_of = weights_x(rank_x_ref, h_ref)
        for j in range(16):
            for i in range(2):
                w_ref[i, j] = jnp.broadcast_to(rows_of[i][:, 2 * j : 2 * j + 1], (8, 128))

    chunk = x_ref.shape[1]
    for r in range(chunk // 8):
        for half in range(2):
            at = (slice(8 * r, 8 * r + 8), slice(128 * half, 128 * half + 128))
            for j in range(16):
                after = x_ref[(2 * j + 2, *at)] if j < 15 else right_ref[at]
                detail_x_ref[(j, *at)] = (
                    x_ref[(2 * j + 1, *at)] - w_ref[0, j] * x_ref[(2 * j, *at)] - w_ref[1, j] * after
                )
    for step in range(chunk // 8):
        rows = slice(step * 8, step * 8 + 8)
        nodes = x_ref[:, rows, :].reshape(256, 256)
        coarse = dot3_left(x_high_ref[...], x_low_ref[...], nodes)
        for k in range(16):
            v_ref[k, rows, :] = (
                coarse[8 * k : 8 * k + 8]
                + x_row_ref[k : k + 1, 0:1] * right_ref[rows, :]
                + x_row_ref[16 + k : 17 + k, 0:1] * left_ref[rows, :]
            )
    values = v_ref[...].reshape(16 * chunk, 256)
    both = dot3(values, high_ref[...], low_ref[...])
    both = both.reshape(16, chunk, 256)
    dz_ref[...] = both[:, :, 0:128]
    cz_ref[...] = both[:, :, 128:256]
    lane = lax.broadcasted_iota(jnp.int32, (chunk, 128), 1)
    message = jnp.zeros((chunk, 128), F32)
    spread = lambda column: jnp.broadcast_to(column, (chunk, 128))
    for k in range(16):
        message = jnp.where(lane == k, spread(v_ref[k, :, 0:1]), message)
        message = jnp.where(lane == 16 + k, spread(dz_ref[k, :, 127:128]), message)
        tail = cz_ref[k, :, 127:128] - v_ref[k, :, 254:255]
        message = jnp.where(lane == 32 + k, spread(tail), message)
    column_ref[...] = message


def carry_kernel(g_ref, one_ref, two_ref, three_ref, high_ref, low_ref, row_ref, column_ref, plane_ref, out_ref):
    carry = two_ref[0:128, :] + two_ref[128:129, :] * three_ref[0:128, :]
    carry = one_ref[0:128, :] + one_ref[128:129, :] * carry
    plane = dot3(carry, high_ref[...], low_ref[...])
    plane_ref[...] = plane
    lane = lax.broadcasted_iota(jnp.int32, (1, 128), 1)
    gain = jnp.zeros((1, 128), F32)
    for k in range(48):
        gain = jnp.where(lane == k, g_ref[k % 16], gain)
    spread = lambda column: jnp.broadcast_to(column, (128, 128))
    wide = lax.broadcasted_iota(jnp.int32, (128, 128), 1)
    pieces = jnp.where(
        wide < 16,
        spread(carry[:, 0:1]),
        jnp.where(wide < 32, spread(plane[:, 127:128]), spread(plane[:, 255:256] - carry[:, 254:255])),
    )
    message = column_ref[...] + gain * pieces
    for i in range(3):
        message = jnp.where(wide == 48 + i, row_ref[4 + i : 5 + i, :], message)
    out_ref[...] = message


def last_kernel(
    rank_ref, g_ref, place_ref, dz_ref, cz_ref, plane_ref, all_ref, row_ref, detail_ref, out_ref
):
    rank = rank_ref[0]

    def clear(i, _):
        out_ref[pl.ds(pl.multiple_of(i * 16, 16), 16)] = jnp.zeros((16, 8, 128), F32)
        return 0

    lax.fori_loop(0, out_ref.shape[0] // 16, clear, 0)
    carry = jnp.zeros((128, 128), F32)
    for r in range(7):
        entering = carry * all_ref[r, 0:1, 50:51] + pltpu.roll(all_ref[r], 96, 1)
        entering = entering + all_ref[r, 0:1, 48:49] * all_ref[r + 1]
        if r > 0:
            entering = entering + all_ref[r, 0:1, 49:50] * pltpu.roll(all_ref[r - 1], 112, 1)
        carry = jnp.where(r < rank, entering, carry)
    right = jnp.where(rank < 7, all_ref[jnp.minimum(rank + 1, 7)], 0.0)
    left = pltpu.roll(all_ref[jnp.maximum(rank - 1, 0)], 112, 1)
    d_right, c_right, c_left, gain = (row_ref[i : i + 1, :] for i in range(4))
    spread = lambda value, k: jnp.broadcast_to(value[:, k : k + 1], (128, 128))
    top = lax.broadcasted_iota(jnp.int32, (8, 128), 0) < 4
    for k in range(16):
        g = g_ref[k]
        right_k = spread(right, k)
        detail = dz_ref[k] + g * plane_ref[:, 0:128] + right_k * d_right
        coarse = cz_ref[k] + g * plane_ref[:, 128:256] + right_k * c_right
        coarse = coarse + spread(left, k) * c_left + spread(carry, k) * gain
        detail_ref[k] = detail
        for i in range(16):
            c8, d8 = coarse[8 * i : 8 * i + 8], detail[8 * i : 8 * i + 8]
            block = 32 * k + 2 * i
            out_ref[place_ref[block]] = jnp.where(top, c8, pltpu.roll(d8, 4, 0))
            out_ref[place_ref[block + 1]] = jnp.where(top, pltpu.roll(c8, 4, 0), d8)


def shift(value, axis, by):
    count = lax.axis_size(axis)
    return lax.ppermute(value, axis, [(i, i + by) for i in range(count) if 0 <= i + by < count])


def local(
    nodal_field, spacing_x, spacing_z, operator_x, persist_x, operator_z, persist_z, receivers
):
    rank_x = lax.axis_index("gx").astype(jnp.int32).reshape(1)
    rank_z = lax.axis_index("gz").astype(jnp.int32).reshape(1)
    plane = jax.ShapeDtypeStruct((128, 256), F32)
    s, v = spec(SMEM), spec(VMEM)

    chunk = 32
    whole = lambda shape: pl.BlockSpec(shape, lambda i: (0,) * len(shape))
    nodes = pl.BlockSpec((32, chunk, 256), lambda i: (0, i, 0))
    thin = pl.BlockSpec((chunk, 256), lambda i: (i, 0))
    third = pl.BlockSpec((16, chunk, 128), lambda i: (0, i, 0))
    grid = (128 // chunk,)
    space_x = spacing_x.reshape(1, 128)

    first, last, own = pl.pallas_call(
        head_kernel,
        grid=grid,
        in_specs=[s, s, whole((1, 128)), nodes],
        out_specs=[thin, thin, thin],
        out_shape=[plane, plane, plane],
        scratch_shapes=[VMEM((33, 8, 128), F32)],
        cost_estimate=cost(64 * 32768, 4 << 20),
        name="head",
    )(rank_x, operator_x, space_x, nodal_field)
    left = shift(last, "gx", 1)
    right = shift(first, "gx", -1)

    near_space = lax.dynamic_slice_in_dim(spacing_z, rank_z[0] * 256, 256)
    square = jax.ShapeDtypeStruct((256, 256), BF16)
    oblong = jax.ShapeDtypeStruct((128, 256), BF16)
    x_high, x_low, x_rows = pl.pallas_call(
        table_x_kernel,
        in_specs=[s, v, v],
        out_specs=[v] * 3,
        out_shape=[oblong, oblong, jax.ShapeDtypeStruct((32, 128), F32)],
        compiler_params=params(),
        cost_estimate=cost(1 << 22, 1 << 17),
        name="table_x",
    )(rank_x, space_x, operator_x)

    ended = pl.pallas_call(
        close_kernel,
        in_specs=[s, v, v, v, v],
        out_specs=v,
        out_shape=jax.ShapeDtypeStruct((136, 256), F32),
        name="close",
    )(persist_x, x_rows, own, right, left)
    one, two, three = (shift(ended, "gx", by) for by in (1, 2, 3))

    high, low, rows = pl.pallas_call(
        table_kernel,
        in_specs=[s, s, v, v, v, v],
        out_specs=[v] * 3,
        out_shape=[square, square, jax.ShapeDtypeStruct((8, 128), F32)],
        compiler_params=params(),
        cost_estimate=cost(12 * 256 * 256 * 128, 1 << 20),
        name="table",
    )(
        rank_z, spacing_z, near_space[0::2].reshape(1, 128), near_space[1::2].reshape(1, 128),
        operator_z, persist_z.reshape(1, 128),
    )

    detail_x, dz, cz, columns = pl.pallas_call(
        main_kernel,
        grid=grid,
        in_specs=[
            s, whole((1, 128)), whole((32, 128)), nodes, thin, thin,
            whole((128, 256)), whole((128, 256)), whole((256, 256)), whole((256, 256)),
        ],
        out_specs=[
            pl.BlockSpec((16, chunk, 256), lambda i: (0, i, 0)),
            third, third, pl.BlockSpec((chunk, 128), lambda i: (i, 0)),
        ],
        out_shape=[
            jax.ShapeDtypeStruct((16, 128, 256), F32),
            jax.ShapeDtypeStruct((16, 128, 128), F32),
            jax.ShapeDtypeStruct((16, 128, 128), F32),
            jax.ShapeDtypeStruct((128, 128), F32),
        ],
        scratch_shapes=[VMEM((16, chunk, 256), F32), VMEM((2, 16, 8, 128), F32)],
        compiler_params=params(),
        cost_estimate=cost(6 * 2048 * 256 * 256, 10 << 20),
        name="main",
    )(rank_x, space_x, x_rows, nodal_field, right, left, x_high, x_low, high, low)

    plane_pass, message = pl.pallas_call(
        carry_kernel,
        in_specs=[s, v, v, v, v, v, v, v],
        out_specs=[v, v],
        out_shape=[plane, jax.ShapeDtypeStruct((128, 128), F32)],
        compiler_params=params(),
        name="carry",
    )(persist_x, one, two, three, high, low, rows, columns)
    gathered = lax.all_gather(message, "gz")

    group = lax.axis_size("gy") * lax.axis_size("gz")
    capacity = 16
    targets = receivers[:, 0]
    positions = jnp.arange(512, dtype=jnp.int32)
    earlier = (targets[None, :] == targets[:, None]) & (positions[None, :] < positions[:, None])
    placed = targets * capacity + jnp.sum(earlier.astype(jnp.int32), axis=1)

    detail_z, outgoing = pl.pallas_call(
        last_kernel,
        in_specs=[s, s, s, v, v, v, v, v],
        out_specs=[v, v],
        out_shape=[
            jax.ShapeDtypeStruct((16, 128, 128), F32),
            jax.ShapeDtypeStruct((group * capacity, 8, 128), F32),
        ],
        compiler_params=params(),
        name="last",
    )(rank_z, persist_x, placed, dz, cz, plane_pass, gathered, rows)
    incoming = lax.all_to_all(
        outgoing.reshape(group, capacity, 8, 128), ("gy", "gz"), split_axis=0, concat_axis=0, tiled=True
    )
    received = incoming.reshape(1, group, capacity, 2, LINES, 128)
    return (detail_x, detail_z, received)


def solution(mesh):
    return jax.shard_map(
        local,
        mesh=mesh,
        in_specs=(
            P("gx", "gy", "gz"),
            P(),
            P(),
            P("gx", None),
            P("gx"),
            P("gz", None),
            P("gz"),
            P(("gx", "gy", "gz"), None),
        ),
        out_specs=(
            P("gx", "gy", "gz"),
            P("gx", "gy", "gz"),
            P(("gx", "gy", "gz"), None, None, None, None, None),
        ),
        check_vma=False,
    )
```

```python
import jax
import jax.numpy as jnp
from jax import lax
from jax.experimental import pallas as pl
from jax.experimental.pallas import tpu as pltpu
from jax.sharding import PartitionSpec as P

LINES = 4
F32 = jnp.float32
BF16 = jnp.bfloat16
SMEM = pltpu.SMEM
VMEM = pltpu.VMEM


def spec(space):
    return pl.BlockSpec(memory_space=space)


def cost(flops, moved):
    return pl.CostEstimate(flops=flops, bytes_accessed=moved, transcendentals=0)


def params(mib=48):
    return pltpu.CompilerParams(vmem_limit_bytes=mib << 20)


def weights_x(rank_ref, h_ref):
    own = pltpu.roll(jnp.broadcast_to(h_ref[...], (8, 128)), 128 - 32 * rank_ref[0], 1)
    after = pltpu.roll(own, 127, 1)
    total = own + after
    return after / total, own / total, 0.5 * own, 0.5 * after


def head_kernel(rank_ref, f_ref, h_ref, x_ref, first_ref, last_ref, out_ref, w_ref):
    @pl.when(pl.program_id(0) == 0)
    def _():
        rows_of = weights_x(rank_ref, h_ref)
        weight = lambda i, k: jnp.broadcast_to(rows_of[i][:, (2 * k) % 128 : (2 * k) % 128 + 1], (8, 128))
        far_before = jnp.where(rank_ref[0] > 0, weight(3, -1), 0.0)
        before = -f_ref[15, 0] * far_before * weight(1, -1)
        for j in range(16):
            v = f_ref[15, j] * weight(2, j)
            if j < 15:
                v = v + f_ref[15, j + 1] * weight(3, j)
            w_ref[2 * j] = before - v * weight(0, j)
            w_ref[2 * j + 1] = v
            before = -v * weight(1, j)
        w_ref[32] = weight(0, 15)

    for r in range(x_ref.shape[1] // 8):
        for half in range(2):
            at = (slice(8 * r, 8 * r + 8), slice(128 * half, 128 * half + 128))
            total = w_ref[0] * x_ref[(0, *at)]
            for x in range(1, 32):
                total = total + w_ref[x] * x_ref[(x, *at)]
            out_ref[at] = total
            first_ref[at] = x_ref[(0, *at)]
            last_ref[at] = x_ref[(31, *at)] - w_ref[32] * x_ref[(30, *at)]


def split(value):
    high = value.astype(BF16)
    return high, (value - high.astype(F32)).astype(BF16)


def dot3(value, high, low):
    v_high, v_low = split(value)
    one = lambda a, b: jnp.dot(a, b, preferred_element_type=F32)
    return one(v_high, high) + (one(v_low, high) + one(v_high, low))


def dot_nt(a, b):
    return lax.dot_general(
        a, b, (((1,), (1,)), ((), ())), precision=lax.Precision.HIGHEST, preferred_element_type=F32
    )


def pass_matrix(even, odd, far_before, b_before, factor, nodes):
    total = even + odd
    a, b = odd / total, even / total
    near, far = 0.5 * even, 0.5 * odd
    z = lax.broadcasted_iota(jnp.int32, (nodes, 128), 0)
    k = lax.broadcasted_iota(jnp.int32, (nodes, 128), 1)
    chosen = jnp.where(z == 2 * k, 1.0, 0.0)
    detail = jnp.where(z == 2 * k + 1, 1.0, 0.0) - chosen * a - jnp.where(z == 2 * k + 2, b, 0.0)
    shifted = jnp.where(k == 0, 0.0, pltpu.roll(detail * far, 1, 1))
    load = detail * near + shifted
    load = load - jnp.where((z == 0) & (k == 0), far_before * b_before, 0.0)
    half = nodes // 2
    return detail, chosen[:, 0:half] + dot_nt(load[:, 0:half], factor), near, b


def table_kernel(rank_ref, h_ref, even_ref, odd_ref, f_ref, g_ref, high_ref, low_ref, row_ref):
    at = jnp.maximum(rank_ref[0] * 256 - 2, 0)
    one = lambda value: jnp.full((1, 1), value, F32)
    h_even, h_odd = one(h_ref[at]), one(h_ref[at + 1])
    far_before = jnp.where(rank_ref[0] > 0, 0.5 * h_odd, 0.0)
    detail, coarse, near, b = pass_matrix(
        even_ref[...], odd_ref[...], far_before, h_even / (h_even + h_odd), f_ref[...], 256
    )
    high, low = split(detail)
    high_ref[:, 0:128], low_ref[:, 0:128] = high, low
    high, low = split(coarse)
    high_ref[:, 128:256], low_ref[:, 128:256] = high, low
    row = lax.broadcasted_iota(jnp.int32, (8, 128), 0)
    lane = lax.broadcasted_iota(jnp.int32, (8, 128), 1)
    pick = jnp.where(((row == 1) & (lane == 127)) | ((row == 2) & (lane == 0)), 1.0, 0.0)
    columns = dot_nt(pick, f_ref[...])
    last = lane[0:1] == 127
    from_right = columns[1:2] * (-near[:, 127:128] * b[:, 127:128])
    from_left = columns[2:3] * far_before
    gain = g_ref[...]
    row_ref[0:1] = jnp.where(last, -b, 0.0)
    row_ref[1:2] = from_right
    row_ref[2:3] = from_left
    row_ref[3:4] = gain
    row_ref[4:5] = jnp.broadcast_to(from_right[:, 127:128], (1, 128))
    row_ref[5:6] = jnp.broadcast_to(from_left[:, 127:128], (1, 128))
    row_ref[6:7] = jnp.broadcast_to(gain[:, 127:128], (1, 128))
    row_ref[7:8] = jnp.zeros((1, 128), F32)


def table_x_kernel(rank_x_ref, hx_ref, fx_ref, x_high_ref, x_low_ref, x_row_ref):
    base = rank_x_ref[0] * 32
    node = lax.broadcasted_iota(jnp.int32, (128, 128), 0)
    place = lax.broadcasted_iota(jnp.int32, (128, 128), 1)
    index = jnp.where(place == 127, jnp.maximum(base - 2, 0), base + 2 * jnp.minimum(place, 15))
    h = jnp.broadcast_to(hx_ref[...], (8, 128))
    take = lambda where: jnp.dot(
        h, jnp.where(node == where, 1.0, 0.0), precision=lax.Precision.HIGHEST, preferred_element_type=F32
    )[0:1]
    even, odd = take(index), take(index + 1)
    far_before = jnp.where(rank_x_ref[0] > 0, 0.5 * odd[:, 127:128], 0.0)
    b_before = even[:, 127:128] / (even[:, 127:128] + odd[:, 127:128])
    factor = fx_ref[...]
    _, coarse, near, b = pass_matrix(even, odd, far_before, b_before, factor, 32)
    one_of = lambda n, m: jnp.where(
        lax.broadcasted_iota(jnp.int32, (n, m), 0) // 8 == lax.broadcasted_iota(jnp.int32, (n, m), 1), 1.0, 0.0
    )
    tall = jnp.dot(
        one_of(256, 32), coarse, precision=lax.Precision.HIGHEST, preferred_element_type=F32
    )
    both = dot_nt(one_of(128, 16), tall)
    same = (
        lax.broadcasted_iota(jnp.int32, (128, 256), 0) % 8
        == lax.broadcasted_iota(jnp.int32, (128, 256), 1) % 8
    )
    high, low = split(jnp.where(same, both, 0.0))
    x_high_ref[...], x_low_ref[...] = high, low
    x_row_ref[0:16, :] = jnp.broadcast_to(factor[:, 15:16] * (-near[:, 15:16] * b[:, 15:16]), (16, 128))
    x_row_ref[16:32, :] = jnp.broadcast_to(factor[:, 0:1] * far_before, (16, 128))


def dot3_left(high, low, value):
    v_high, v_low = split(value)
    one = lambda a, b: jnp.dot(a, b, preferred_element_type=F32)
    return one(high, v_high) + (one(high, v_low) + one(low, v_high))


def main_kernel(
    rank_x_ref, h_ref, x_row_ref, x_ref, right_ref, left_ref, x_high_ref, x_low_ref, high_ref, low_ref,
    detail_x_ref, dz_ref, cz_ref, column_ref, v_ref, w_ref,
):
    @pl.when(pl.program_id(0) == 0)
    def _():
        rows_of = weights_x(rank_x_ref, h_ref)
        for j in range(16):
            for i in range(2):
                w_ref[i, j] = jnp.broadcast_to(rows_of[i][:, 2 * j : 2 * j + 1], (8, 128))

    chunk = x_ref.shape[1]
    for r in range(chunk // 8):
        for half in range(2):
            at = (slice(8 * r, 8 * r + 8), slice(128 * half, 128 * half + 128))
            for j in range(16):
                after = x_ref[(2 * j + 2, *at)] if j < 15 else right_ref[at]
                detail_x_ref[(j, *at)] = (
                    x_ref[(2 * j + 1, *at)] - w_ref[0, j] * x_ref[(2 * j, *at)] - w_ref[1, j] * after
                )
    for step in range(chunk // 8):
        rows = slice(step * 8, step * 8 + 8)
        nodes = x_ref[:, rows, :].reshape(256, 256)
        coarse = dot3_left(x_high_ref[...], x_low_ref[...], nodes)
        for k in range(16):
            v_ref[k, rows, :] = (
                coarse[8 * k : 8 * k + 8]
                + x_row_ref[k : k + 1, 0:1] * right_ref[rows, :]
                + x_row_ref[16 + k : 17 + k, 0:1] * left_ref[rows, :]
            )
    values = v_ref[...].reshape(16 * chunk, 256)
    both = dot3(values, high_ref[...], low_ref[...])
    both = both.reshape(16, chunk, 256)
    dz_ref[...] = both[:, :, 0:128]
    cz_ref[...] = both[:, :, 128:256]
    lane = lax.broadcasted_iota(jnp.int32, (chunk, 128), 1)
    message = jnp.zeros((chunk, 128), F32)
    spread = lambda column: jnp.broadcast_to(column, (chunk, 128))
    for k in range(16):
        message = jnp.where(lane == k, spread(v_ref[k, :, 0:1]), message)
        message = jnp.where(lane == 16 + k, spread(dz_ref[k, :, 127:128]), message)
        tail = cz_ref[k, :, 127:128] - v_ref[k, :, 254:255]
        message = jnp.where(lane == 32 + k, spread(tail), message)
    column_ref[...] = message


def carry_kernel(g_ref, one_ref, two_ref, three_ref, high_ref, low_ref, row_ref, column_ref, plane_ref, out_ref):
    carry = two_ref[0:128, :] + two_ref[128:129, :] * three_ref[0:128, :]
    carry = one_ref[0:128, :] + one_ref[128:129, :] * carry
    plane = dot3(carry, high_ref[...], low_ref[...])
    plane_ref[...] = plane
    lane = lax.broadcasted_iota(jnp.int32, (1, 128), 1)
    gain = jnp.zeros((1, 128), F32)
    for k in range(48):
        gain = jnp.where(lane == k, g_ref[k % 16], gain)
    spread = lambda column: jnp.broadcast_to(column, (128, 128))
    wide = lax.broadcasted_iota(jnp.int32, (128, 128), 1)
    pieces = jnp.where(
        wide < 16,
        spread(carry[:, 0:1]),
        jnp.where(wide < 32, spread(plane[:, 127:128]), spread(plane[:, 255:256] - carry[:, 254:255])),
    )
    message = column_ref[...] + gain * pieces
    for i in range(3):
        message = jnp.where(wide == 48 + i, row_ref[4 + i : 5 + i, :], message)
    out_ref[...] = message


def last_kernel(
    rank_ref, g_ref, place_ref, dz_ref, cz_ref, plane_ref, all_ref, row_ref, detail_ref, out_ref
):
    rank = rank_ref[0]

    def clear(i, _):
        out_ref[pl.ds(pl.multiple_of(i * 16, 16), 16)] = jnp.zeros((16, 8, 128), F32)
        return 0

    lax.fori_loop(0, out_ref.shape[0] // 16, clear, 0)
    carry = jnp.zeros((128, 128), F32)
    for r in range(7):
        entering = carry * all_ref[r, 0:1, 50:51] + pltpu.roll(all_ref[r], 96, 1)
        entering = entering + all_ref[r, 0:1, 48:49] * all_ref[r + 1]
        if r > 0:
            entering = entering + all_ref[r, 0:1, 49:50] * pltpu.roll(all_ref[r - 1], 112, 1)
        carry = jnp.where(r < rank, entering, carry)
    right = jnp.where(rank < 7, all_ref[jnp.minimum(rank + 1, 7)], 0.0)
    left = pltpu.roll(all_ref[jnp.maximum(rank - 1, 0)], 112, 1)
    d_right, c_right, c_left, gain = (row_ref[i : i + 1, :] for i in range(4))
    spread = lambda value, k: jnp.broadcast_to(value[:, k : k + 1], (128, 128))
    top = lax.broadcasted_iota(jnp.int32, (8, 128), 0) < 4
    for k in range(16):
        g = g_ref[k]
        right_k = spread(right, k)
        detail = dz_ref[k] + g * plane_ref[:, 0:128] + right_k * d_right
        coarse = cz_ref[k] + g * plane_ref[:, 128:256] + right_k * c_right
        coarse = coarse + spread(left, k) * c_left + spread(carry, k) * gain
        detail_ref[k] = detail
        for i in range(16):
            c8, d8 = coarse[8 * i : 8 * i + 8], detail[8 * i : 8 * i + 8]
            block = 32 * k + 2 * i
            out_ref[place_ref[block]] = jnp.where(top, c8, pltpu.roll(d8, 4, 0))
            out_ref[place_ref[block + 1]] = jnp.where(top, pltpu.roll(c8, 4, 0), d8)


def shift(value, axis, by):
    count = lax.axis_size(axis)
    return lax.ppermute(value, axis, [(i, i + by) for i in range(count) if 0 <= i + by < count])


def local(
    nodal_field, spacing_x, spacing_z, operator_x, persist_x, operator_z, persist_z, receivers
):
    rank_x = lax.axis_index("gx").astype(jnp.int32).reshape(1)
    rank_z = lax.axis_index("gz").astype(jnp.int32).reshape(1)
    plane = jax.ShapeDtypeStruct((128, 256), F32)
    s, v = spec(SMEM), spec(VMEM)

    chunk = 32
    whole = lambda shape: pl.BlockSpec(shape, lambda i: (0,) * len(shape))
    nodes = pl.BlockSpec((32, chunk, 256), lambda i: (0, i, 0))
    thin = pl.BlockSpec((chunk, 256), lambda i: (i, 0))
    third = pl.BlockSpec((16, chunk, 128), lambda i: (0, i, 0))
    grid = (128 // chunk,)
    space_x = spacing_x.reshape(1, 128)

    first, last, own = pl.pallas_call(
        head_kernel,
        grid=grid,
        in_specs=[s, s, whole((1, 128)), nodes],
        out_specs=[thin, thin, thin],
        out_shape=[plane, plane, plane],
        scratch_shapes=[VMEM((33, 8, 128), F32)],
        cost_estimate=cost(64 * 32768, 4 << 20),
        name="head",
    )(rank_x, operator_x, space_x, nodal_field)
    left = shift(last, "gx", 1)
    right = shift(first, "gx", -1)

    near_space = lax.dynamic_slice_in_dim(spacing_z, rank_z[0] * 256, 256)
    square = jax.ShapeDtypeStruct((256, 256), BF16)
    oblong = jax.ShapeDtypeStruct((128, 256), BF16)
    x_high, x_low, x_rows = pl.pallas_call(
        table_x_kernel,
        in_specs=[s, v, v],
        out_specs=[v] * 3,
        out_shape=[oblong, oblong, jax.ShapeDtypeStruct((32, 128), F32)],
        compiler_params=params(),
        cost_estimate=cost(1 << 22, 1 << 17),
        name="table_x",
    )(rank_x, space_x, operator_x)

    total = own + x_rows[15:16, 0:1] * right + x_rows[31:32, 0:1] * left
    ended = jnp.concatenate([total, jnp.broadcast_to(persist_x[15], (8, 256))], axis=0)
    one, two, three = (shift(ended, "gx", by) for by in (1, 2, 3))

    high, low, rows = pl.pallas_call(
        table_kernel,
        in_specs=[s, s, v, v, v, v],
        out_specs=[v] * 3,
        out_shape=[square, square, jax.ShapeDtypeStruct((8, 128), F32)],
        compiler_params=params(),
        cost_estimate=cost(12 * 256 * 256 * 128, 1 << 20),
        name="table",
    )(
        rank_z, spacing_z, near_space[0::2].reshape(1, 128), near_space[1::2].reshape(1, 128),
        operator_z, persist_z.reshape(1, 128),
    )

    detail_x, dz, cz, columns = pl.pallas_call(
        main_kernel,
        grid=grid,
        in_specs=[
            s, whole((1, 128)), whole((32, 128)), nodes, thin, thin,
            whole((128, 256)), whole((128, 256)), whole((256, 256)), whole((256, 256)),
        ],
        out_specs=[
            pl.BlockSpec((16, chunk, 256), lambda i: (0, i, 0)),
            third, third, pl.BlockSpec((chunk, 128), lambda i: (i, 0)),
        ],
        out_shape=[
            jax.ShapeDtypeStruct((16, 128, 256), F32),
            jax.ShapeDtypeStruct((16, 128, 128), F32),
            jax.ShapeDtypeStruct((16, 128, 128), F32),
            jax.ShapeDtypeStruct((128, 128), F32),
        ],
        scratch_shapes=[VMEM((16, chunk, 256), F32), VMEM((2, 16, 8, 128), F32)],
        compiler_params=params(),
        cost_estimate=cost(6 * 2048 * 256 * 256, 10 << 20),
        name="main",
    )(rank_x, space_x, x_rows, nodal_field, right, left, x_high, x_low, high, low)

    plane_pass, message = pl.pallas_call(
        carry_kernel,
        in_specs=[s, v, v, v, v, v, v, v],
        out_specs=[v, v],
        out_shape=[plane, jax.ShapeDtypeStruct((128, 128), F32)],
        compiler_params=params(),
        name="carry",
    )(persist_x, one, two, three, high, low, rows, columns)
    gathered = lax.all_gather(message, "gz")

    group = lax.axis_size("gy") * lax.axis_size("gz")
    capacity = 16
    targets = receivers[:, 0]
    positions = jnp.arange(512, dtype=jnp.int32)
    earlier = (targets[None, :] == targets[:, None]) & (positions[None, :] < positions[:, None])
    placed = targets * capacity + jnp.sum(earlier.astype(jnp.int32), axis=1)

    detail_z, outgoing = pl.pallas_call(
        last_kernel,
        in_specs=[s, s, s, v, v, v, v, v],
        out_specs=[v, v],
        out_shape=[
            jax.ShapeDtypeStruct((16, 128, 128), F32),
            jax.ShapeDtypeStruct((group * capacity, 8, 128), F32),
        ],
        compiler_params=params(),
        name="last",
    )(rank_z, persist_x, placed, dz, cz, plane_pass, gathered, rows)
    incoming = lax.all_to_all(
        outgoing.reshape(group, capacity, 8, 128), ("gy", "gz"), split_axis=0, concat_axis=0, tiled=True
    )
    received = incoming.reshape(1, group, capacity, 2, LINES, 128)
    return (detail_x, detail_z, received)


def solution(mesh):
    return jax.shard_map(
        local,
        mesh=mesh,
        in_specs=(
            P("gx", "gy", "gz"),
            P(),
            P(),
            P("gx", None),
            P("gx"),
            P("gz", None),
            P("gz"),
            P(("gx", "gy", "gz"), None),
        ),
        out_specs=(
            P("gx", "gy", "gz"),
            P("gx", "gy", "gz"),
            P(("gx", "gy", "gz"), None, None, None, None, None),
        ),
        check_vma=False,
    )
```

```python
import jax
import jax.numpy as jnp
from jax import lax
from jax.experimental import pallas as pl
from jax.experimental.pallas import tpu as pltpu
from jax.sharding import PartitionSpec as P

LINES = 4
F32 = jnp.float32
BF16 = jnp.bfloat16
SMEM = pltpu.SMEM
VMEM = pltpu.VMEM


def spec(space):
    return pl.BlockSpec(memory_space=space)


def cost(flops, moved):
    return pl.CostEstimate(flops=flops, bytes_accessed=moved, transcendentals=0)


def params(mib=48):
    return pltpu.CompilerParams(vmem_limit_bytes=mib << 20)


def weights_x(rank_ref, h_ref):
    own = pltpu.roll(jnp.broadcast_to(h_ref[...], (8, 128)), 128 - 32 * rank_ref[0], 1)
    after = pltpu.roll(own, 127, 1)
    total = own + after
    return after / total, own / total, 0.5 * own, 0.5 * after


def head_kernel(rank_ref, f_ref, h_ref, x_ref, first_ref, last_ref, out_ref, w_ref):
    @pl.when(pl.program_id(0) == 0)
    def _():
        rows_of = weights_x(rank_ref, h_ref)
        weight = lambda i, k: jnp.broadcast_to(rows_of[i][:, (2 * k) % 128 : (2 * k) % 128 + 1], (8, 128))
        far_before = jnp.where(rank_ref[0] > 0, weight(3, -1), 0.0)
        before = -f_ref[15, 0] * far_before * weight(1, -1)
        for j in range(16):
            v = f_ref[15, j] * weight(2, j)
            if j < 15:
                v = v + f_ref[15, j + 1] * weight(3, j)
            w_ref[2 * j] = before - v * weight(0, j)
            w_ref[2 * j + 1] = v
            before = -v * weight(1, j)
        w_ref[32] = weight(0, 15)

    for r in range(x_ref.shape[1] // 8):
        for half in range(2):
            at = (slice(8 * r, 8 * r + 8), slice(128 * half, 128 * half + 128))
            total = w_ref[0] * x_ref[(0, *at)]
            for x in range(1, 32):
                total = total + w_ref[x] * x_ref[(x, *at)]
            out_ref[at] = total
            first_ref[at] = x_ref[(0, *at)]
            last_ref[at] = x_ref[(31, *at)] - w_ref[32] * x_ref[(30, *at)]


def split(value):
    high = value.astype(BF16)
    return high, (value - high.astype(F32)).astype(BF16)


def dot3(value, high, low):
    v_high, v_low = split(value)
    one = lambda a, b: jnp.dot(a, b, preferred_element_type=F32)
    return one(v_high, high) + (one(v_low, high) + one(v_high, low))


def dot_nt(a, b):
    return lax.dot_general(
        a, b, (((1,), (1,)), ((), ())), precision=lax.Precision.HIGHEST, preferred_element_type=F32
    )


def pass_matrix(even, odd, far_before, b_before, factor, nodes):
    total = even + odd
    a, b = odd / total, even / total
    near, far = 0.5 * even, 0.5 * odd
    z = lax.broadcasted_iota(jnp.int32, (nodes, 128), 0)
    k = lax.broadcasted_iota(jnp.int32, (nodes, 128), 1)
    chosen = jnp.where(z == 2 * k, 1.0, 0.0)
    detail = jnp.where(z == 2 * k + 1, 1.0, 0.0) - chosen * a - jnp.where(z == 2 * k + 2, b, 0.0)
    shifted = jnp.where(k == 0, 0.0, pltpu.roll(detail * far, 1, 1))
    load = detail * near + shifted
    load = load - jnp.where((z == 0) & (k == 0), far_before * b_before, 0.0)
    half = nodes // 2
    return detail, chosen[:, 0:half] + dot_nt(load[:, 0:half], factor), near, b


def table_kernel(rank_ref, h_ref, even_ref, odd_ref, f_ref, g_ref, high_ref, low_ref, row_ref):
    at = jnp.maximum(rank_ref[0] * 256 - 2, 0)
    one = lambda value: jnp.full((1, 1), value, F32)
    h_even, h_odd = one(h_ref[at]), one(h_ref[at + 1])
    far_before = jnp.where(rank_ref[0] > 0, 0.5 * h_odd, 0.0)
    detail, coarse, near, b = pass_matrix(
        even_ref[...], odd_ref[...], far_before, h_even / (h_even + h_odd), f_ref[...], 256
    )
    high, low = split(detail)
    high_ref[:, 0:128], low_ref[:, 0:128] = high, low
    high, low = split(coarse)
    high_ref[:, 128:256], low_ref[:, 128:256] = high, low
    row = lax.broadcasted_iota(jnp.int32, (8, 128), 0)
    lane = lax.broadcasted_iota(jnp.int32, (8, 128), 1)
    pick = jnp.where(((row == 1) & (lane == 127)) | ((row == 2) & (lane == 0)), 1.0, 0.0)
    columns = dot_nt(pick, f_ref[...])
    last = lane[0:1] == 127
    from_right = columns[1:2] * (-near[:, 127:128] * b[:, 127:128])
    from_left = columns[2:3] * far_before
    gain = g_ref[...]
    row_ref[0:1] = jnp.where(last, -b, 0.0)
    row_ref[1:2] = from_right
    row_ref[2:3] = from_left
    row_ref[3:4] = gain
    row_ref[4:5] = jnp.broadcast_to(from_right[:, 127:128], (1, 128))
    row_ref[5:6] = jnp.broadcast_to(from_left[:, 127:128], (1, 128))
    row_ref[6:7] = jnp.broadcast_to(gain[:, 127:128], (1, 128))
    row_ref[7:8] = jnp.zeros((1, 128), F32)


def table_x_kernel(rank_x_ref, g_ref, hx_ref, fx_ref, x_high_ref, x_low_ref, x_row_ref, end_ref):
    base = rank_x_ref[0] * 32
    node = lax.broadcasted_iota(jnp.int32, (128, 128), 0)
    place = lax.broadcasted_iota(jnp.int32, (128, 128), 1)
    index = jnp.where(place == 127, jnp.maximum(base - 2, 0), base + 2 * jnp.minimum(place, 15))
    h = jnp.broadcast_to(hx_ref[...], (8, 128))
    take = lambda where: jnp.dot(
        h, jnp.where(node == where, 1.0, 0.0), precision=lax.Precision.HIGHEST, preferred_element_type=F32
    )[0:1]
    even, odd = take(index), take(index + 1)
    far_before = jnp.where(rank_x_ref[0] > 0, 0.5 * odd[:, 127:128], 0.0)
    b_before = even[:, 127:128] / (even[:, 127:128] + odd[:, 127:128])
    factor = fx_ref[...]
    _, coarse, near, b = pass_matrix(even, odd, far_before, b_before, factor, 32)
    one_of = lambda n, m: jnp.where(
        lax.broadcasted_iota(jnp.int32, (n, m), 0) // 8 == lax.broadcasted_iota(jnp.int32, (n, m), 1), 1.0, 0.0
    )
    tall = jnp.dot(
        one_of(256, 32), coarse, precision=lax.Precision.HIGHEST, preferred_element_type=F32
    )
    both = dot_nt(one_of(128, 16), tall)
    same = (
        lax.broadcasted_iota(jnp.int32, (128, 256), 0) % 8
        == lax.broadcasted_iota(jnp.int32, (128, 256), 1) % 8
    )
    high, low = split(jnp.where(same, both, 0.0))
    x_high_ref[...], x_low_ref[...] = high, low
    x_row_ref[0:16, :] = jnp.broadcast_to(factor[:, 15:16] * (-near[:, 15:16] * b[:, 15:16]), (16, 128))
    x_row_ref[16:32, :] = jnp.broadcast_to(factor[:, 0:1] * far_before, (16, 128))
    end_ref[0:8, :] = jnp.broadcast_to(x_row_ref[15:16, 0:1], (8, 256))
    end_ref[8:16, :] = jnp.broadcast_to(x_row_ref[31:32, 0:1], (8, 256))
    end_ref[16:24, :] = jnp.full((8, 256), g_ref[15], F32)


def dot3_left(high, low, value):
    v_high, v_low = split(value)
    one = lambda a, b: jnp.dot(a, b, preferred_element_type=F32)
    return one(high, v_high) + (one(high, v_low) + one(low, v_high))


def main_kernel(
    rank_x_ref, h_ref, x_row_ref, x_ref, right_ref, left_ref, x_high_ref, x_low_ref, high_ref, low_ref,
    detail_x_ref, dz_ref, cz_ref, column_ref, v_ref, w_ref,
):
    @pl.when(pl.program_id(0) == 0)
    def _():
        rows_of = weights_x(rank_x_ref, h_ref)
        for j in range(16):
            for i in range(2):
                w_ref[i, j] = jnp.broadcast_to(rows_of[i][:, 2 * j : 2 * j + 1], (8, 128))

    chunk = x_ref.shape[1]
    for r in range(chunk // 8):
        for half in range(2):
            at = (slice(8 * r, 8 * r + 8), slice(128 * half, 128 * half + 128))
            for j in range(16):
                after = x_ref[(2 * j + 2, *at)] if j < 15 else right_ref[at]
                detail_x_ref[(j, *at)] = (
                    x_ref[(2 * j + 1, *at)] - w_ref[0, j] * x_ref[(2 * j, *at)] - w_ref[1, j] * after
                )
    for step in range(chunk // 8):
        rows = slice(step * 8, step * 8 + 8)
        nodes = x_ref[:, rows, :].reshape(256, 256)
        coarse = dot3_left(x_high_ref[...], x_low_ref[...], nodes)
        for k in range(16):
            v_ref[k, rows, :] = (
                coarse[8 * k : 8 * k + 8]
                + x_row_ref[k : k + 1, 0:1] * right_ref[rows, :]
                + x_row_ref[16 + k : 17 + k, 0:1] * left_ref[rows, :]
            )
    values = v_ref[...].reshape(16 * chunk, 256)
    both = dot3(values, high_ref[...], low_ref[...])
    both = both.reshape(16, chunk, 256)
    dz_ref[...] = both[:, :, 0:128]
    cz_ref[...] = both[:, :, 128:256]
    lane = lax.broadcasted_iota(jnp.int32, (chunk, 128), 1)
    message = jnp.zeros((chunk, 128), F32)
    spread = lambda column: jnp.broadcast_to(column, (chunk, 128))
    for k in range(16):
        message = jnp.where(lane == k, spread(v_ref[k, :, 0:1]), message)
        message = jnp.where(lane == 16 + k, spread(dz_ref[k, :, 127:128]), message)
        tail = cz_ref[k, :, 127:128] - v_ref[k, :, 254:255]
        message = jnp.where(lane == 32 + k, spread(tail), message)
    column_ref[...] = message


def carry_kernel(g_ref, one_ref, two_ref, three_ref, high_ref, low_ref, row_ref, column_ref, plane_ref, out_ref):
    carry = two_ref[0:128, :] + two_ref[128:129, :] * three_ref[0:128, :]
    carry = one_ref[0:128, :] + one_ref[128:129, :] * carry
    plane = dot3(carry, high_ref[...], low_ref[...])
    plane_ref[...] = plane
    lane = lax.broadcasted_iota(jnp.int32, (1, 128), 1)
    gain = jnp.zeros((1, 128), F32)
    for k in range(48):
        gain = jnp.where(lane == k, g_ref[k % 16], gain)
    spread = lambda column: jnp.broadcast_to(column, (128, 128))
    wide = lax.broadcasted_iota(jnp.int32, (128, 128), 1)
    pieces = jnp.where(
        wide < 16,
        spread(carry[:, 0:1]),
        jnp.where(wide < 32, spread(plane[:, 127:128]), spread(plane[:, 255:256] - carry[:, 254:255])),
    )
    message = column_ref[...] + gain * pieces
    for i in range(3):
        message = jnp.where(wide == 48 + i, row_ref[4 + i : 5 + i, :], message)
    out_ref[...] = message


def last_kernel(
    rank_ref, g_ref, place_ref, dz_ref, cz_ref, plane_ref, all_ref, row_ref, detail_ref, out_ref
):
    rank = rank_ref[0]

    def clear(i, _):
        out_ref[pl.ds(pl.multiple_of(i * 16, 16), 16)] = jnp.zeros((16, 8, 128), F32)
        return 0

    lax.fori_loop(0, out_ref.shape[0] // 16, clear, 0)
    carry = jnp.zeros((128, 128), F32)
    for r in range(7):
        entering = carry * all_ref[r, 0:1, 50:51] + pltpu.roll(all_ref[r], 96, 1)
        entering = entering + all_ref[r, 0:1, 48:49] * all_ref[r + 1]
        if r > 0:
            entering = entering + all_ref[r, 0:1, 49:50] * pltpu.roll(all_ref[r - 1], 112, 1)
        carry = jnp.where(r < rank, entering, carry)
    right = jnp.where(rank < 7, all_ref[jnp.minimum(rank + 1, 7)], 0.0)
    left = pltpu.roll(all_ref[jnp.maximum(rank - 1, 0)], 112, 1)
    d_right, c_right, c_left, gain = (row_ref[i : i + 1, :] for i in range(4))
    spread = lambda value, k: jnp.broadcast_to(value[:, k : k + 1], (128, 128))
    top = lax.broadcasted_iota(jnp.int32, (8, 128), 0) < 4
    for k in range(16):
        g = g_ref[k]
        right_k = spread(right, k)
        detail = dz_ref[k] + g * plane_ref[:, 0:128] + right_k * d_right
        coarse = cz_ref[k] + g * plane_ref[:, 128:256] + right_k * c_right
        coarse = coarse + spread(left, k) * c_left + spread(carry, k) * gain
        detail_ref[k] = detail
        for i in range(16):
            c8, d8 = coarse[8 * i : 8 * i + 8], detail[8 * i : 8 * i + 8]
            block = 32 * k + 2 * i
            out_ref[place_ref[block]] = jnp.where(top, c8, pltpu.roll(d8, 4, 0))
            out_ref[place_ref[block + 1]] = jnp.where(top, pltpu.roll(c8, 4, 0), d8)


def shift(value, axis, by):
    count = lax.axis_size(axis)
    return lax.ppermute(value, axis, [(i, i + by) for i in range(count) if 0 <= i + by < count])


def local(
    nodal_field, spacing_x, spacing_z, operator_x, persist_x, operator_z, persist_z, receivers
):
    rank_x = lax.axis_index("gx").astype(jnp.int32).reshape(1)
    rank_z = lax.axis_index("gz").astype(jnp.int32).reshape(1)
    plane = jax.ShapeDtypeStruct((128, 256), F32)
    s, v = spec(SMEM), spec(VMEM)

    chunk = 32
    whole = lambda shape: pl.BlockSpec(shape, lambda i: (0,) * len(shape))
    nodes = pl.BlockSpec((32, chunk, 256), lambda i: (0, i, 0))
    thin = pl.BlockSpec((chunk, 256), lambda i: (i, 0))
    third = pl.BlockSpec((16, chunk, 128), lambda i: (0, i, 0))
    grid = (128 // chunk,)
    space_x = spacing_x.reshape(1, 128)

    first, last, own = pl.pallas_call(
        head_kernel,
        grid=grid,
        in_specs=[s, s, whole((1, 128)), nodes],
        out_specs=[thin, thin, thin],
        out_shape=[plane, plane, plane],
        scratch_shapes=[VMEM((33, 8, 128), F32)],
        cost_estimate=cost(64 * 32768, 4 << 20),
        name="head",
    )(rank_x, operator_x, space_x, nodal_field)
    left = shift(last, "gx", 1)
    right = shift(first, "gx", -1)

    near_space = lax.dynamic_slice_in_dim(spacing_z, rank_z[0] * 256, 256)
    square = jax.ShapeDtypeStruct((256, 256), BF16)
    oblong = jax.ShapeDtypeStruct((128, 256), BF16)
    x_high, x_low, x_rows, ends = pl.pallas_call(
        table_x_kernel,
        in_specs=[s, s, v, v],
        out_specs=[v] * 4,
        out_shape=[
            oblong, oblong, jax.ShapeDtypeStruct((32, 128), F32), jax.ShapeDtypeStruct((24, 256), F32),
        ],
        compiler_params=params(),
        cost_estimate=cost(1 << 22, 1 << 17),
        name="table_x",
    )(rank_x, persist_x, space_x, operator_x)

    total = own + ends[0:1] * right + ends[8:9] * left
    ended = jnp.concatenate([total, ends[16:24]], axis=0)
    one, two, three = (shift(ended, "gx", by) for by in (1, 2, 3))

    high, low, rows = pl.pallas_call(
        table_kernel,
        in_specs=[s, s, v, v, v, v],
        out_specs=[v] * 3,
        out_shape=[square, square, jax.ShapeDtypeStruct((8, 128), F32)],
        compiler_params=params(),
        cost_estimate=cost(12 * 256 * 256 * 128, 1 << 20),
        name="table",
    )(
        rank_z, spacing_z, near_space[0::2].reshape(1, 128), near_space[1::2].reshape(1, 128),
        operator_z, persist_z.reshape(1, 128),
    )

    detail_x, dz, cz, columns = pl.pallas_call(
        main_kernel,
        grid=grid,
        in_specs=[
            s, whole((1, 128)), whole((32, 128)), nodes, thin, thin,
            whole((128, 256)), whole((128, 256)), whole((256, 256)), whole((256, 256)),
        ],
        out_specs=[
            pl.BlockSpec((16, chunk, 256), lambda i: (0, i, 0)),
            third, third, pl.BlockSpec((chunk, 128), lambda i: (i, 0)),
        ],
        out_shape=[
            jax.ShapeDtypeStruct((16, 128, 256), F32),
            jax.ShapeDtypeStruct((16, 128, 128), F32),
            jax.ShapeDtypeStruct((16, 128, 128), F32),
            jax.ShapeDtypeStruct((128, 128), F32),
        ],
        scratch_shapes=[VMEM((16, chunk, 256), F32), VMEM((2, 16, 8, 128), F32)],
        compiler_params=params(),
        cost_estimate=cost(6 * 2048 * 256 * 256, 10 << 20),
        name="main",
    )(rank_x, space_x, x_rows, nodal_field, right, left, x_high, x_low, high, low)

    plane_pass, message = pl.pallas_call(
        carry_kernel,
        in_specs=[s, v, v, v, v, v, v, v],
        out_specs=[v, v],
        out_shape=[plane, jax.ShapeDtypeStruct((128, 128), F32)],
        compiler_params=params(),
        name="carry",
    )(persist_x, one, two, three, high, low, rows, columns)
    gathered = lax.all_gather(message, "gz")

    group = lax.axis_size("gy") * lax.axis_size("gz")
    capacity = 16
    targets = receivers[:, 0]
    positions = jnp.arange(512, dtype=jnp.int32)
    earlier = (targets[None, :] == targets[:, None]) & (positions[None, :] < positions[:, None])
    placed = targets * capacity + jnp.sum(earlier.astype(jnp.int32), axis=1)

    detail_z, outgoing = pl.pallas_call(
        last_kernel,
        in_specs=[s, s, s, v, v, v, v, v],
        out_specs=[v, v],
        out_shape=[
            jax.ShapeDtypeStruct((16, 128, 128), F32),
            jax.ShapeDtypeStruct((group * capacity, 8, 128), F32),
        ],
        compiler_params=params(),
        name="last",
    )(rank_z, persist_x, placed, dz, cz, plane_pass, gathered, rows)
    incoming = lax.all_to_all(
        outgoing.reshape(group, capacity, 8, 128), ("gy", "gz"), split_axis=0, concat_axis=0, tiled=True
    )
    received = incoming.reshape(1, group, capacity, 2, LINES, 128)
    return (detail_x, detail_z, received)


def solution(mesh):
    return jax.shard_map(
        local,
        mesh=mesh,
        in_specs=(
            P("gx", "gy", "gz"),
            P(),
            P(),
            P("gx", None),
            P("gx"),
            P("gz", None),
            P("gz"),
            P(("gx", "gy", "gz"), None),
        ),
        out_specs=(
            P("gx", "gy", "gz"),
            P("gx", "gy", "gz"),
            P(("gx", "gy", "gz"), None, None, None, None, None),
        ),
        check_vma=False,
    )
```
